256 devices in a mesh: rows: 32 (over y, x, core), cols: 8 (over z).
Axes of the slice: x: 4, y: 4, z: 8, core: 2. Of those that a mesh axis runs over, the one named last changes fastest.
Arguments:
- anomalies: bfloat16 [131072, 64], P(('rows', 'cols')), may hold values from -6 to 6
- innovations: bfloat16 [131072, 64], P(('rows', 'cols')), may hold values from -3 to 3
- pair_rows: int32 [32, 8192], P('rows', 'cols'), may hold values from 0 to 31, as said below
- pair_cols: int32 [32, 8192], P('rows', 'cols'), may hold values from 0 to 127
- pair_dist: int32 [32, 8192], P('rows', 'cols'), may hold values from 0 to 7
- pair_counts: int32 [32, 8], P('rows', 'cols'), may hold values from 128 to 1024, as said below
Outputs:
- increment: float32 [131072, 64], P(('rows', 'cols'))
The draws below stay inside these ranges and needn't reach their ends.
Inputs may be any that keep to these rules, and one draw needn't show every extreme that they name: In the 1024 slots of one device the pairs (pair_rows, pair_cols) are distinct, and each row block stands in at most 32 of them. `pair_counts`: some device has all its slots live in every draw.
All inputs are finite; a program needn't handle non-finite values.
Results may differ from the reference program's by a relative error of at most 0.005.
Values may be sent and summed in bfloat16 or wider, within the bound.
A program may use at most 128 MiB of HBM per device.

```python
import jax
import jax.numpy as jnp
from jax import lax

BLK = 128
M = 64
K = 64
TAPER_CELLS = 8
DMAX = 8
CELL_DEV = 512
PAIRS_BLOCK = 32
RBLK = 32
CBLK = 128
P_DEV = 1024
NCELLS = 131072
N_ROWS = 32
N_COLS = 8


def slot_pairs(key):
    device_total = N_ROWS * N_COLS
    perm_key = jax.random.fold_in(key, 11)
    shuffle_key = jax.random.fold_in(key, 17)
    perm_keys = jax.random.split(perm_key, device_total * RBLK)
    col_perms = jax.vmap(lambda one_key: jax.random.permutation(one_key, CBLK))(perm_keys)
    chosen = col_perms[:, :PAIRS_BLOCK].reshape(device_total, P_DEV)
    row_table = jnp.repeat(jnp.arange(RBLK), PAIRS_BLOCK)
    row_table = jnp.broadcast_to(row_table[None, :], (device_total, P_DEV))
    shuffle_keys = jax.random.split(shuffle_key, device_total)
    orders = jax.vmap(lambda one_key: jax.random.permutation(one_key, P_DEV))(shuffle_keys)
    row_out = jnp.take_along_axis(row_table, orders, axis=1)
    col_out = jnp.take_along_axis(chosen, orders, axis=1)
    return (row_out.reshape(N_ROWS, N_COLS * P_DEV).astype(jnp.int32), col_out.reshape(N_ROWS, N_COLS * P_DEV).astype(jnp.int32))


def draw_pair_rows(key, part):
    return slot_pairs(key)[0]


def draw_pair_cols(key, part):
    return slot_pairs(key)[1]


def draw_pair_counts(key, part):
    base_key = jax.random.fold_in(key, 29)
    flame_key, high_key, low_key, top_key = jax.random.split(base_key, 4)
    flame = jax.random.randint(flame_key, (), 0, N_ROWS)
    row_index = jnp.arange(N_ROWS)[:, None]
    col_index = jnp.arange(N_COLS)[None, :]
    apart = jnp.abs(row_index - flame)
    cycle_apart = jnp.minimum(apart, N_ROWS - apart)
    near_flame = cycle_apart <= N_ROWS // 8
    high_load = jax.random.randint(high_key, (N_ROWS, N_COLS), P_DEV // 2, P_DEV + 1)
    low_load = jax.random.randint(low_key, (N_ROWS, N_COLS), P_DEV // 8, P_DEV // 3 + 1)
    loads = jnp.where(near_flame, high_load, low_load)
    top_col = jax.random.randint(top_key, (), 0, N_COLS)
    loads = jnp.where((row_index == flame) & (col_index == top_col), P_DEV, loads)
    return loads.astype(jnp.int32)


def touch_ends(entries, rng, low, high):
    longest = entries.shape.index(max(entries.shape))
    spots = []
    for shift in (0, 1):
        where = [jax.random.randint(jax.random.fold_in(rng, axis), (), 0, length) for axis, length in enumerate(entries.shape)]
        where[longest] = (where[longest] + shift) % entries.shape[longest]
        spots.append(tuple(where))
    return entries.at[spots[0]].set(low).at[spots[1]].set(high)


def level_of(stream_key, extent, pieces, low, high):
    factor_of, own = 1.0, jax.random.fold_in(stream_key, 6)
    for dim, blocks in pieces:
        steps = jnp.exp(jax.random.uniform(jax.random.fold_in(own, dim), (blocks,), jnp.float32, low / len(pieces), high / len(pieces)))
        factor_of = factor_of * jnp.repeat(steps, extent[dim] // blocks).reshape([-1 if axis == dim else 1 for axis in range(len(extent))])
    return factor_of


def bell_draw(key, shape, spread, bound, shards=(), kind=jnp.bfloat16):
    values = jax.random.normal(key, shape, jnp.float32) * spread
    if len(shards) > 0:
        values = level_of(key, shape, shards, -0.22, 0.18) * values
    return jnp.clip(values, min=-bound, max=bound).astype(kind)


def setup_inputs(seed: int = 0) -> dict:
    streams_of = jax.random.split(jax.random.key(seed), 7)
    return {
        "anomalies": bell_draw(streams_of[0], (NCELLS, M), 1.0, 6.0, ((0, 256),)),
        "innovations": bell_draw(streams_of[1], (NCELLS, K), 0.5, 3.0, ((0, 256),)),
        "pair_rows": draw_pair_rows(jax.random.fold_in(streams_of[6], 71), 0),
        "pair_cols": draw_pair_cols(jax.random.fold_in(streams_of[6], 71), 0),
        "pair_dist": touch_ends(jax.random.randint(streams_of[4], (N_ROWS, N_COLS * P_DEV), 0, DMAX), jax.random.fold_in(streams_of[4], 1), 0, DMAX - 1).astype(jnp.int32),
        "pair_counts": draw_pair_counts(jax.random.fold_in(streams_of[6], 71), 0),
    }


DIST_SCALE = 4.0


def reference(anomalies, innovations, pair_rows, pair_cols, pair_dist, pair_counts):
    per_dev = CELL_DEV // BLK
    anom_blocks = anomalies.reshape(NCELLS // BLK, BLK, M)
    innov_blocks = innovations.reshape(NCELLS // BLK, BLK, K)
    offsets = jnp.arange(BLK)
    kernel = jnp.exp(-jnp.abs(offsets[:, None] - offsets[None, :]).astype(jnp.float32) / TAPER_CELLS)
    row_ids = pair_rows.reshape(N_ROWS * N_COLS, P_DEV)
    col_ids = pair_cols.reshape(N_ROWS * N_COLS, P_DEV)
    distances = pair_dist.reshape(N_ROWS * N_COLS, P_DEV)
    live_counts = pair_counts.reshape(N_ROWS * N_COLS)
    slot_index = jnp.arange(P_DEV)
    block_index = jnp.arange(RBLK)

    def device_part(device):
        row_index = device // N_COLS
        col_range = device % N_COLS
        local_rows = row_ids[device]
        col_local = col_ids[device]
        first_blocks = row_index * RBLK + local_rows
        second_blocks = (col_local // per_dev) * RBLK + col_range * per_dev + col_local % per_dev
        live_slot = slot_index < live_counts[device]
        left = anom_blocks[first_blocks].astype(jnp.float32)
        right = anom_blocks[second_blocks].astype(jnp.float32)
        innov = innov_blocks[second_blocks].astype(jnp.float32)
        products = jnp.einsum('pim,pjm->pij', left, right)
        block_weight = jnp.where(live_slot, jnp.exp(-distances[device].astype(jnp.float32) / DIST_SCALE), 0.0)
        tapered = (products * (1.0 / (M - 1)) * block_weight[:, None, None] * kernel).astype(jnp.bfloat16)
        applied = jnp.einsum('pij,pjk->pik', tapered.astype(jnp.float32), innov)
        onehot = (local_rows[:, None] == block_index[None, :]).astype(jnp.float32)
        return jnp.einsum('pr,pik->rik', onehot, applied)

    partials = lax.map(device_part, jnp.arange(N_ROWS * N_COLS))
    summed = partials.reshape(N_ROWS, N_COLS, RBLK * BLK, K).sum(axis=1)
    return summed.reshape(NCELLS, K)
```

```python
import functools
import math

import jax
import jax.numpy as jnp
from jax import lax
from jax.experimental import pallas as pl
from jax.experimental.pallas import tpu as pltpu
from jax.sharding import PartitionSpec as P

BLK = 128
SLOTS = 32
TAPER_CELLS = 8
DIST_SCALE = 4.0
DISTS = 8
NY, NX, NZ = 4, 4, 8
MESH = pl.DeviceIdType.MESH
F32, BF16 = jnp.float32, jnp.bfloat16


def slot_lists(rows, cols, dist, count, col_blocks):
    slots = rows.shape[1]
    chunks = range(slots // BLK)
    live = lax.broadcasted_iota(jnp.int32, (1, slots), 1) < count
    held = jnp.where(live, rows, 2 * slots)
    entry = (dist + 1) * col_blocks + cols
    lane = lax.broadcasted_iota(jnp.int32, (BLK, BLK), 1)
    earlier = lax.broadcasted_iota(jnp.int32, (BLK, BLK), 0) < lane

    def part(v, c):
        return v[:, c * BLK : (c + 1) * BLK]

    def down(v, c):
        return jnp.broadcast_to(part(v, c), (BLK, BLK)).T

    held_down = [down(held, c) for c in chunks]
    places = []
    for c in chunks:
        same = jnp.where((held_down[c] == part(held, c)) & earlier, 1, 0)
        for e in range(c):
            same = same + jnp.where(held_down[e] == part(held, c), 1, 0)
        places.append(part(held, c) * SLOTS + jnp.sum(same, axis=0, keepdims=True))
    place = jnp.concatenate(places, axis=1)
    place_down = [down(place, c) for c in chunks]
    entry_down = [down(entry, c) for c in chunks]
    out = []
    for c in chunks:
        found = jnp.zeros((BLK, BLK), jnp.int32)
        for e in chunks:
            found = found + jnp.where(place_down[e] == lane + c * BLK, entry_down[e], 0)
        out.append(jnp.sum(found, axis=0, keepdims=True))
    return jnp.concatenate(out, axis=1)


def kernel(
    count_ref, x_ref, v_ref, rows_ref, cols_ref, dist_ref, out_ref,
    col, row, taper, lists, list_smem, part, own, landed,
    send_sem, recv_sem, rs_send, rs_recv, local_sem,
):
    r, z = lax.axis_index("rows"), lax.axis_index("cols")
    core = lax.rem(r, 2)
    chip = r // 2
    x, y = lax.rem(chip, NX), chip // NX
    members, cells = x_ref.shape
    half = cells // BLK // 2

    def dev(yy, xx):
        return (lax.rem(yy + NY, NY) * NX + lax.rem(xx + NX, NX)) * 2 + core

    def slab(dy, dx, s):
        return (lax.rem(y + dy + NY, NY) * NX + lax.rem(x + dx + NX, NX)) * 2 + s

    sib = r + 1 - 2 * core

    group_rows = cells // BLK
    mine = []
    for n, (src, dst) in enumerate(((x_ref, col.at[0, r]), (v_ref, col.at[1, r]), (x_ref, row.at[z]))):
        for b in range(group_rows):
            mine.append(
                pltpu.make_async_copy(
                    src.at[:, b * BLK : (b + 1) * BLK], dst.at[b], local_sem.at[n * group_rows + b]
                )
            )
    for c in mine:
        c.start()

    barrier = pltpu.get_barrier_semaphore()
    peers = [(sib, z), (dev(y, x + 1), z), (dev(y, x - 1), z), (dev(y + 1, x), z), (dev(y - 1, x), z)]
    peers += [(r, lax.rem(z + k, NZ)) for k in range(1, NZ)]
    for peer in peers:
        pl.semaphore_signal(barrier, inc=1, device_id=peer, device_id_type=MESH)
    for c in mine:
        c.wait()
    pl.semaphore_wait(barrier, len(peers))

    started = []

    def push(src, device, k):
        c = pltpu.make_async_remote_copy(
            src_ref=src, dst_ref=src, send_sem=send_sem.at[k], recv_sem=recv_sem.at[k],
            device_id=device, device_id_type=MESH,
        )
        c.start()
        started.append(c)
        return c

    counter = iter(range(1000))

    def key():
        return next(counter)

    class Kind:
        def __init__(self, other):
            self.s = 1 - core if other else core
            self.fy = self.s
            self.fx = 1 - self.s

        def first(self, d):
            return (dev(y + d * self.fy, x + d * self.fx), z)

        def second(self, d):
            return (dev(y + d * self.fx, x + d * self.fy), z)

        def at(self, o, e):
            return slab(o * self.fy + e * self.fx, o * self.fx + e * self.fy, self.s)

    kinds = [Kind(False), Kind(True)]

    def full(k, o, e):
        return col.at[core, k.at(o, e)]

    def halved(k, o, e, h):
        return col.at[core, k.at(o, e), pl.ds(h * half, half)]

    sib_copies = []

    def to_sib(k, o, e):
        sib_copies.append(push(full(k, o, e), (sib, z), key()))

    ev = {}
    swap = push(col.at[1 - core, r], (sib, z), key())
    own_kind, other_kind = kinds

    def begin(i):
        k = kinds[i]
        for d in (1, -1):
            ev[i, "f", d] = push(full(k, 0, 0), k.first(d), key())
        for d in (1, -1):
            ev[i, "s", 0, d] = push(full(k, 0, 0), k.second(d), key())

    begin(0)
    zev = {}
    zev[1, 1] = push(row.at[z], (r, lax.rem(z + 1, NZ)), key())
    zev[1, -1] = push(row.at[z], (r, lax.rem(z + NZ - 1, NZ)), key())
    to_sib(own_kind, 0, 0)
    swap.wait_recv()
    begin(1)

    i = lax.broadcasted_iota(jnp.int32, (BLK, BLK), 0)
    j = lax.broadcasted_iota(jnp.int32, (BLK, BLK), 1)
    base = jnp.exp(-jnp.abs(i - j).astype(F32) / TAPER_CELLS) * (1.0 / (members - 1))
    taper[0] = jnp.zeros((BLK, BLK), F32)
    for d in range(DISTS):
        taper[d + 1] = base * math.exp(-d / DIST_SCALE)
    col_blocks = col.shape[1] * group_rows
    lists[...] = slot_lists(rows_ref[...], cols_ref[...], dist_ref[...], count_ref[0, 0], col_blocks)
    to_smem = pltpu.make_async_copy(lists, list_smem, local_sem.at[3 * group_rows])
    to_smem.start()

    def zrelay(step):
        for d in (1, -1):
            zev[step, d].wait_recv()
            where = lax.rem(z - d * step + NZ, NZ)
            target = (r, lax.rem(z + d + NZ, NZ))
            if step + 1 < NZ // 2:
                zev[step + 1, d] = push(row.at[where], target, key())
            elif step + 1 == NZ // 2:
                h = 0 if d == 1 else 1
                zev[step + 1, d] = push(row.at[where, pl.ds(h * half, half)], target, key())

    for n, k in enumerate(kinds):
        for d in (1, -1):
            ev[n, "f", d].wait_recv()
            h = 0 if d == 1 else 1
            ev[n, "ff", d] = push(halved(k, -d, 0, h), k.first(d), key())
            for e in (1, -1):
                ev[n, "s", -d, e] = push(full(k, -d, 0), k.second(e), key())
            to_sib(k, -d, 0)
    zrelay(1)
    for n, k in enumerate(kinds):
        for e in (1, -1):
            ev[n, "s", 0, e].wait_recv()
            h = 0 if e == 1 else 1
            ev[n, "sf", 0, e] = push(halved(k, 0, -e, h), k.second(e), key())
            to_sib(k, 0, -e)
    for n, k in enumerate(kinds):
        ev[n, "ff", 1].wait_recv()
        ev[n, "ff", -1].wait_recv()
        for e in (1, -1):
            ev[n, "s", 2, e] = push(full(k, 2, 0), k.second(e), key())
        to_sib(k, 2, 0)
    zrelay(2)
    for o in (-1, 1, 2):
        for n, k in enumerate(kinds):
            for e in (1, -1):
                ev[n, "s", o, e].wait_recv()
                h = 0 if e == 1 else 1
                ev[n, "sf", o, e] = push(halved(k, o, -e, h), k.second(e), key())
                to_sib(k, o, -e)
        if o == -1:
            zrelay(3)
    for o in (0, -1, 1, 2):
        for n, k in enumerate(kinds):
            for e in (1, -1):
                ev[n, "sf", o, e].wait_recv()
            to_sib(k, o, 2)
    for d in (1, -1):
        zev[NZ // 2, d].wait_recv()
    to_smem.wait()
    for c in sib_copies:
        c.wait_recv()

    nt = (((1,), (1,)), ((), ()))

    def entry(a, s):
        e = list_smem[0, a * SLOTS + s]
        q = e & (col_blocks - 1)
        return e // col_blocks, q // group_rows, q & (group_rows - 1)

    def one_block(a, xa):
        total = None
        for s in range(0, SLOTS, 2):
            d0, q0, b0 = entry(a, s)
            d1, q1, b1 = entry(a, s + 1)
            xb = jnp.concatenate([col[0, q0, b0], col[0, q1, b1]], axis=1)
            prod = jnp.dot(xa, xb, preferred_element_type=F32)
            kd = jnp.concatenate([taper[d0], taper[d1]], axis=1)
            t = (prod * kd).astype(BF16)
            vb = jnp.concatenate([col[1, q0, b0], col[1, q1, b1]], axis=1)
            term = lax.dot_general(t, vb, nt, preferred_element_type=F32)
            total = term if total is None else total + term
        return total

    @pl.loop(0, NZ)
    def _(t):
        off = NZ // 2 + (t + 1) // 2 * (1 - 2 * lax.rem(t, 2))
        g = lax.rem(z + off, NZ)

        @pl.loop(0, group_rows)
        def _(b):
            xa = row[g, b].astype(F32).T.astype(BF16)
            y_t = one_block(g * group_rows + b, xa).T
            own[b] = y_t
            part[t, b] = y_t.astype(BF16)

        @pl.when(t < NZ - 1)
        def _():
            pltpu.make_async_remote_copy(
                src_ref=part.at[t], dst_ref=landed.at[t], send_sem=rs_send.at[t], recv_sem=rs_recv.at[t],
                device_id=(r, g), device_id_type=MESH,
            ).start()

    total = own[...]
    for t in range(NZ - 1):
        done = pltpu.make_async_remote_copy(
            src_ref=part.at[t], dst_ref=landed.at[t], send_sem=rs_send.at[t], recv_sem=rs_recv.at[t],
            device_id=(r, lax.rem(z + 1, NZ)), device_id_type=MESH,
        )
        done.wait()
        total = total + landed[t].astype(F32)
    for b in range(group_rows):
        out_ref[:, b * BLK : (b + 1) * BLK] = total[b]
    for c in started:
        c.wait_send()


def local(anomalies, innovations, pair_rows, pair_cols, pair_dist, pair_counts):
    cells, members = anomalies.shape
    columns = innovations.shape[1]
    n_rows = lax.axis_size("rows")
    vm = pl.BlockSpec(memory_space=pltpu.VMEM)
    hbm = pl.BlockSpec(memory_space=pl.ANY)
    each = cells // BLK
    blocks = NZ * each
    out = pl.pallas_call(
        kernel,
        out_shape=jax.ShapeDtypeStruct((columns, cells), F32),
        in_specs=[pl.BlockSpec(memory_space=pltpu.SMEM), hbm, hbm, vm, vm, vm],
        out_specs=vm,
        scratch_shapes=[
            pltpu.VMEM((2, n_rows, each, members, BLK), BF16),
            pltpu.VMEM((NZ, each, members, BLK), BF16),
            pltpu.VMEM((DISTS + 1, BLK, BLK), F32),
            pltpu.VMEM((1, blocks * SLOTS), jnp.int32),
            pltpu.SMEM((1, blocks * SLOTS), jnp.int32),
            pltpu.VMEM((NZ, each, columns, BLK), BF16),
            pltpu.VMEM((each, columns, BLK), F32),
            pltpu.VMEM((NZ - 1, each, columns, BLK), BF16),
            pltpu.SemaphoreType.DMA((96,)),
            pltpu.SemaphoreType.DMA((96,)),
            pltpu.SemaphoreType.DMA((NZ - 1,)),
            pltpu.SemaphoreType.DMA((NZ - 1,)),
            pltpu.SemaphoreType.DMA((3 * each + 1,)),
        ],
        compiler_params=pltpu.CompilerParams(
            collective_id=0, has_side_effects=True, vmem_limit_bytes=48 << 20
        ),
        name="increment",
    )(pair_counts, anomalies.T, innovations.T, pair_rows, pair_cols, pair_dist)
    return out.T


def solution(mesh):
    split = P(("rows", "cols"), None)
    pairs = P("rows", "cols")
    return jax.shard_map(
        local, mesh=mesh, in_specs=(split, split, pairs, pairs, pairs, pairs), out_specs=split, check_vma=False
    )
```

```python
import functools
import math

import jax
import jax.numpy as jnp
from jax import lax
from jax.experimental import pallas as pl
from jax.experimental.pallas import tpu as pltpu
from jax.sharding import PartitionSpec as P

BLK = 128
SLOTS = 32
GROUP = 8
TAPER_CELLS = 8
DIST_SCALE = 4.0
DISTS = 8
NY, NX, NZ = 4, 4, 8
MESH = pl.DeviceIdType.MESH
F32, BF16 = jnp.float32, jnp.bfloat16


def slot_lists(rows, cols, dist, count, col_blocks):
    slots = rows.shape[1]
    chunks = range(slots // BLK)
    live = lax.broadcasted_iota(jnp.int32, (1, slots), 1) < count
    held = jnp.where(live, rows, 2 * slots)
    entry = (dist + 1) * col_blocks + cols
    lane = lax.broadcasted_iota(jnp.int32, (BLK, BLK), 1)
    earlier = lax.broadcasted_iota(jnp.int32, (BLK, BLK), 0) < lane

    def part(v, c):
        return v[:, c * BLK : (c + 1) * BLK]

    def down(v, c):
        return jnp.broadcast_to(part(v, c), (BLK, BLK)).T

    held_down = [down(held, c) for c in chunks]
    places = []
    for c in chunks:
        same = jnp.where((held_down[c] == part(held, c)) & earlier, 1, 0)
        for e in range(c):
            same = same + jnp.where(held_down[e] == part(held, c), 1, 0)
        places.append(part(held, c) * SLOTS + jnp.sum(same, axis=0, keepdims=True))
    place = jnp.concatenate(places, axis=1)
    place_down = [down(place, c) for c in chunks]
    entry_down = [down(entry, c) for c in chunks]
    out = []
    for c in chunks:
        found = jnp.zeros((BLK, BLK), jnp.int32)
        for e in chunks:
            found = found + jnp.where(place_down[e] == lane + c * BLK, entry_down[e], 0)
        out.append(jnp.sum(found, axis=0, keepdims=True))
    return jnp.concatenate(out, axis=1)


def kernel(
    count_ref, x_ref, v_ref, rows_ref, cols_ref, dist_ref, out_ref,
    count, pairs, col, row, taper, lists, list_smem, part, own, landed,
    send_sem, recv_sem, rs_send, rs_recv, local_sem,
):
    r, z = lax.axis_index("rows"), lax.axis_index("cols")
    core = lax.rem(r, 2)
    chip = r // 2
    x, y = lax.rem(chip, NX), chip // NX
    members, cells = x_ref.shape
    half = cells // BLK // 2

    def dev(yy, xx):
        return (lax.rem(yy + NY, NY) * NX + lax.rem(xx + NX, NX)) * 2 + core

    def slab(dy, dx, s):
        return (lax.rem(y + dy + NY, NY) * NX + lax.rem(x + dx + NX, NX)) * 2 + s

    sib = r + 1 - 2 * core

    group_rows = cells // BLK
    mine = []
    for n, (src, dst) in enumerate(((x_ref, col.at[0, r]), (v_ref, col.at[1, r]), (x_ref, row.at[z]))):
        for b in range(group_rows):
            mine.append(
                pltpu.make_async_copy(
                    src.at[:, b * BLK : (b + 1) * BLK], dst.at[b], local_sem.at[n * group_rows + b]
                )
            )
    for c in mine:
        c.start()
    listed = [pltpu.make_async_copy(count_ref, count, local_sem.at[3 * group_rows])]
    for n, ref in enumerate((rows_ref, cols_ref, dist_ref)):
        listed.append(pltpu.make_async_copy(ref, pairs.at[n], local_sem.at[3 * group_rows + 1 + n]))
    for c in listed:
        c.start()

    barrier = pltpu.get_barrier_semaphore()
    peers = [(sib, z), (dev(y, x + 1), z), (dev(y, x - 1), z), (dev(y + 1, x), z), (dev(y - 1, x), z)]
    peers += [(r, lax.rem(z + k, NZ)) for k in range(1, NZ)]
    for peer in peers:
        pl.semaphore_signal(barrier, inc=1, device_id=peer, device_id_type=MESH)
    for c in mine:
        c.wait()
    pl.semaphore_wait(barrier, len(peers))

    started = []

    def push(src, device, k):
        c = pltpu.make_async_remote_copy(
            src_ref=src, dst_ref=src, send_sem=send_sem.at[k], recv_sem=recv_sem.at[k],
            device_id=device, device_id_type=MESH,
        )
        c.start()
        started.append(c)
        return c

    counter = iter(range(1000))

    def key():
        return next(counter)

    class Kind:
        def __init__(self, other):
            self.s = 1 - core if other else core
            self.fy = self.s
            self.fx = 1 - self.s

        def first(self, d):
            return (dev(y + d * self.fy, x + d * self.fx), z)

        def second(self, d):
            return (dev(y + d * self.fx, x + d * self.fy), z)

        def at(self, o, e):
            return slab(o * self.fy + e * self.fx, o * self.fx + e * self.fy, self.s)

    kinds = [Kind(False), Kind(True)]

    def full(k, o, e):
        return col.at[core, k.at(o, e)]

    def halved(k, o, e, h):
        return col.at[core, k.at(o, e), pl.ds(h * half, half)]

    sib_copies = []

    def to_sib(k, o, e):
        sib_copies.append(push(full(k, o, e), (sib, z), key()))

    ev = {}
    swap = push(col.at[1 - core, r], (sib, z), key())
    own_kind, other_kind = kinds

    def begin(i):
        k = kinds[i]
        for d in (1, -1):
            ev[i, "f", d] = push(full(k, 0, 0), k.first(d), key())
        for d in (1, -1):
            ev[i, "s", 0, d] = push(full(k, 0, 0), k.second(d), key())

    begin(0)
    zev = {}
    zev[1, 1] = push(row.at[z], (r, lax.rem(z + 1, NZ)), key())
    zev[1, -1] = push(row.at[z], (r, lax.rem(z + NZ - 1, NZ)), key())
    to_sib(own_kind, 0, 0)
    swap.wait_recv()
    begin(1)

    i = lax.broadcasted_iota(jnp.int32, (BLK, BLK), 0)
    j = lax.broadcasted_iota(jnp.int32, (BLK, BLK), 1)
    base = jnp.exp(-jnp.abs(i - j).astype(F32) / TAPER_CELLS) * (1.0 / (members - 1))
    taper[0] = jnp.zeros((BLK, BLK), F32)
    for d in range(DISTS):
        taper[d + 1] = base * math.exp(-d / DIST_SCALE)
    col_blocks = col.shape[1] * group_rows
    for c in listed:
        c.wait()
    lists[...] = slot_lists(pairs[0], pairs[1], pairs[2], count[0, 0], col_blocks)
    to_smem = pltpu.make_async_copy(lists, list_smem, local_sem.at[3 * group_rows + 4])
    to_smem.start()

    def zrelay(step):
        for d in (1, -1):
            zev[step, d].wait_recv()
            where = lax.rem(z - d * step + NZ, NZ)
            target = (r, lax.rem(z + d + NZ, NZ))
            if step + 1 < NZ // 2:
                zev[step + 1, d] = push(row.at[where], target, key())
            elif step + 1 == NZ // 2:
                h = 0 if d == 1 else 1
                zev[step + 1, d] = push(row.at[where, pl.ds(h * half, half)], target, key())

    for n, k in enumerate(kinds):
        for d in (1, -1):
            ev[n, "f", d].wait_recv()
            h = 0 if d == 1 else 1
            ev[n, "ff", d] = push(halved(k, -d, 0, h), k.first(d), key())
            for e in (1, -1):
                ev[n, "s", -d, e] = push(full(k, -d, 0), k.second(e), key())
            to_sib(k, -d, 0)
    zrelay(1)
    for n, k in enumerate(kinds):
        for e in (1, -1):
            ev[n, "s", 0, e].wait_recv()
            h = 0 if e == 1 else 1
            ev[n, "sf", 0, e] = push(halved(k, 0, -e, h), k.second(e), key())
            to_sib(k, 0, -e)
    for n, k in enumerate(kinds):
        ev[n, "ff", 1].wait_recv()
        ev[n, "ff", -1].wait_recv()
        for e in (1, -1):
            ev[n, "s", 2, e] = push(full(k, 2, 0), k.second(e), key())
        to_sib(k, 2, 0)
    zrelay(2)
    for o in (-1, 1, 2):
        for n, k in enumerate(kinds):
            for e in (1, -1):
                ev[n, "s", o, e].wait_recv()
                h = 0 if e == 1 else 1
                ev[n, "sf", o, e] = push(halved(k, o, -e, h), k.second(e), key())
                to_sib(k, o, -e)
        if o == -1:
            zrelay(3)
    for o in (0, -1, 1, 2):
        for n, k in enumerate(kinds):
            for e in (1, -1):
                ev[n, "sf", o, e].wait_recv()
            to_sib(k, o, 2)
    for d in (1, -1):
        zev[NZ // 2, d].wait_recv()
    to_smem.wait()
    for c in sib_copies:
        c.wait_recv()

    tn = (((0,), (0,)), ((), ()))

    def entry(a, s):
        e = list_smem[0, a * SLOTS + s]
        q = e & (col_blocks - 1)
        return e // col_blocks, q // group_rows, q & (group_rows - 1)

    @pl.loop(0, NZ)
    def _(t):
        off = NZ // 2 + (t + 1) // 2 * (1 - 2 * lax.rem(t, 2))
        g = lax.rem(z + off, NZ)
        turns = SLOTS // GROUP
        steps = turns * group_rows
        products, tapered, sums = {}, {}, {}
        for i in range(steps + 2):
            if i < steps:
                b = i // turns
                xa = row[g, b]
                entries = [entry(g * group_rows + b, i % turns * GROUP + n) for n in range(GROUP)]
                products[i] = entries, [
                    lax.dot_general(col[0, q, k], xa, tn, preferred_element_type=F32) for _, q, k in entries
                ]
            if 1 <= i <= steps:
                entries, prods = products.pop(i - 1)
                tapered[i - 1] = entries, jnp.concatenate(
                    [(p * taper[d]).astype(BF16) for p, (d, _, _) in zip(prods, entries)], axis=0
                )
            if i >= 2:
                b, turn = divmod(i - 2, turns)
                entries, weights = tapered.pop(i - 2)
                vb = jnp.concatenate([col[1, q, k] for _, q, k in entries], axis=1)
                term = jnp.dot(vb, weights, preferred_element_type=F32)
                sums[b] = term if turn == 0 else sums[b] + term
                if turn == turns - 1:
                    done = sums.pop(b)
                    own[b] = done
                    part[t, b] = done.astype(BF16)

        @pl.when(t < NZ - 1)
        def _():
            pltpu.make_async_remote_copy(
                src_ref=part.at[t], dst_ref=landed.at[t], send_sem=rs_send.at[t], recv_sem=rs_recv.at[t],
                device_id=(r, g), device_id_type=MESH,
            ).start()

    total = own[...]
    for t in range(NZ - 1):
        done = pltpu.make_async_remote_copy(
            src_ref=part.at[t], dst_ref=landed.at[t], send_sem=rs_send.at[t], recv_sem=rs_recv.at[t],
            device_id=(r, lax.rem(z + 1, NZ)), device_id_type=MESH,
        )
        done.wait()
        total = total + landed[t].astype(F32)
    for b in range(group_rows):
        out_ref[:, b * BLK : (b + 1) * BLK] = total[b]
    for c in started:
        c.wait_send()


def local(anomalies, innovations, pair_rows, pair_cols, pair_dist, pair_counts):
    cells, members = anomalies.shape
    columns = innovations.shape[1]
    n_rows = lax.axis_size("rows")
    vm = pl.BlockSpec(memory_space=pltpu.VMEM)
    hbm = pl.BlockSpec(memory_space=pltpu.HBM)
    each = cells // BLK
    blocks = NZ * each
    out = pl.pallas_call(
        kernel,
        out_shape=jax.ShapeDtypeStruct((columns, cells), F32),
        in_specs=[hbm] * 6,
        out_specs=vm,
        scratch_shapes=[
            pltpu.SMEM(pair_counts.shape, jnp.int32),
            pltpu.VMEM((3,) + pair_rows.shape, jnp.int32),
            pltpu.VMEM((2, n_rows, each, members, BLK), BF16),
            pltpu.VMEM((NZ, each, members, BLK), BF16),
            pltpu.VMEM((DISTS + 1, BLK, BLK), F32),
            pltpu.VMEM((1, blocks * SLOTS), jnp.int32),
            pltpu.SMEM((1, blocks * SLOTS), jnp.int32),
            pltpu.VMEM((NZ, each, columns, BLK), BF16),
            pltpu.VMEM((each, columns, BLK), F32),
            pltpu.VMEM((NZ - 1, each, columns, BLK), BF16),
            pltpu.SemaphoreType.DMA((96,)),
            pltpu.SemaphoreType.DMA((96,)),
            pltpu.SemaphoreType.DMA((NZ - 1,)),
            pltpu.SemaphoreType.DMA((NZ - 1,)),
            pltpu.SemaphoreType.DMA((3 * each + 5,)),
        ],
        compiler_params=pltpu.CompilerParams(
            collective_id=0, has_side_effects=True, vmem_limit_bytes=48 << 20
        ),
        name="increment",
    )(pair_counts, anomalies.T, innovations.T, pair_rows, pair_cols, pair_dist)
    return out.T


def solution(mesh):
    split = P(("rows", "cols"), None)
    pairs = P("rows", "cols")
    return jax.shard_map(
        local, mesh=mesh, in_specs=(split, split, pairs, pairs, pairs, pairs), out_specs=split, check_vma=False
    )
```

```python
import functools
import math

import jax
import jax.numpy as jnp
from jax import lax
from jax.experimental import pallas as pl
from jax.experimental.pallas import tpu as pltpu
from jax.sharding import PartitionSpec as P

BLK = 128
SLOTS = 32
GROUP = 8
TAPER_CELLS = 8
DIST_SCALE = 4.0
DISTS = 8
NY, NX, NZ = 4, 4, 8
MESH = pl.DeviceIdType.MESH
RING = (1, -1, 2)
F32, BF16 = jnp.float32, jnp.bfloat16


def slot_lists(rows, cols, dist, count, col_blocks):
    slots = rows.shape[1]
    chunks = range(slots // BLK)
    live = lax.broadcasted_iota(jnp.int32, (1, slots), 1) < count
    held = jnp.where(live, rows, 2 * slots)
    entry = (dist + 1) * col_blocks + cols
    lane = lax.broadcasted_iota(jnp.int32, (BLK, BLK), 1)
    earlier = lax.broadcasted_iota(jnp.int32, (BLK, BLK), 0) < lane

    def part(v, c):
        return v[:, c * BLK : (c + 1) * BLK]

    def down(v, c):
        return jnp.broadcast_to(part(v, c), (BLK, BLK)).T

    held_down = [down(held, c) for c in chunks]
    places = []
    for c in chunks:
        same = jnp.where((held_down[c] == part(held, c)) & earlier, 1, 0)
        for e in range(c):
            same = same + jnp.where(held_down[e] == part(held, c), 1, 0)
        places.append(part(held, c) * SLOTS + jnp.sum(same, axis=0, keepdims=True))
    place = jnp.concatenate(places, axis=1)
    place_down = [down(place, c) for c in chunks]
    entry_down = [down(entry, c) for c in chunks]
    out = []
    for c in chunks:
        found = jnp.zeros((BLK, BLK), jnp.int32)
        for e in chunks:
            found = found + jnp.where(place_down[e] == lane + c * BLK, entry_down[e], 0)
        out.append(jnp.sum(found, axis=0, keepdims=True))
    return jnp.concatenate(out, axis=1)


def kernel(
    count_ref, x_ref, v_ref, rows_ref, cols_ref, dist_ref, out_ref,
    count, pairs, col, row, taper, lists, list_smem, part, own, landed,
    send_sem, recv_sem, rs_send, rs_recv, local_sem, ready,
):
    r, z = lax.axis_index("rows"), lax.axis_index("cols")
    core = lax.rem(r, 2)
    chip = r // 2
    x, y = lax.rem(chip, NX), chip // NX
    members, cells = x_ref.shape

    def dev(yy, xx):
        return (lax.rem(yy + NY, NY) * NX + lax.rem(xx + NX, NX)) * 2 + core

    sib = r + 1 - 2 * core

    group_rows = cells // BLK
    mine = []
    for n, (src, dst) in enumerate(((x_ref, col.at[0, r]), (v_ref, col.at[1, r]), (x_ref, row.at[z]))):
        for b in range(group_rows):
            mine.append(
                pltpu.make_async_copy(
                    src.at[:, b * BLK : (b + 1) * BLK], dst.at[b], local_sem.at[n * group_rows + b]
                )
            )
    for c in mine:
        c.start()
    listed = [pltpu.make_async_copy(count_ref, count, local_sem.at[3 * group_rows])]
    for n, ref in enumerate((rows_ref, cols_ref, dist_ref)):
        listed.append(pltpu.make_async_copy(ref, pairs.at[n], local_sem.at[3 * group_rows + 1 + n]))
    for c in listed:
        c.start()

    barrier = pltpu.get_barrier_semaphore()
    peers = [(sib, z)]
    peers += [(dev(y, x + d), z) for d in RING] + [(dev(y + d, x), z) for d in RING]
    for peer in peers:
        pl.semaphore_signal(barrier, inc=1, device_id=peer, device_id_type=MESH)
    for k in range(1, NZ):
        @pl.when(z + k < NZ)
        def _():
            pl.semaphore_signal(barrier, inc=1, device_id=(r, lax.rem(z + k, NZ)), device_id_type=MESH)

    for c in mine:
        c.wait()
    pl.semaphore_wait(barrier, len(peers) + z)
    for k in range(1, NZ):
        @pl.when(z + k >= NZ)
        def _():
            pl.semaphore_signal(ready, inc=1, device_id=(r, lax.rem(z + k, NZ)), device_id_type=MESH)

    started = []

    def copy(src, device, k):
        c = pltpu.make_async_remote_copy(
            src_ref=src, dst_ref=src, send_sem=send_sem.at[k], recv_sem=recv_sem.at[k],
            device_id=device, device_id_type=MESH,
        )
        started.append(c)
        return c

    def push(src, device, k):
        c = copy(src, device, k)
        c.start()
        return c

    counter = iter(range(1000))

    def key():
        return next(counter)

    def place(n, o, e):
        return dev(y + (o if n else e), x + (e if n else o))

    def slab(n, o, e):
        return col.at[n, place(n, o, e)]

    ev = {}
    sib_copies = []

    def to_sib(n, o, e):
        sib_copies.append(push(slab(n, o, e), (sib, z), key()))

    def along_second(n, o):
        for e in RING:
            ev[n, o, e] = push(slab(n, o, 0), (place(n, 0, e), z), key())

    for d in RING:
        for n in range(2):
            ev[n, d] = push(slab(n, 0, 0), (place(n, d, 0), z), key())
    for n in range(2):
        along_second(n, 0)
    zev = [copy(row.at[z], (r, lax.rem(z + k, NZ)), key()) for k in range(1, NZ)]
    for k in range(1, NZ):
        @pl.when(z + k >= NZ)
        def _():
            zev[k - 1].start()

    for n in range(2):
        to_sib(n, 0, 0)

    i = lax.broadcasted_iota(jnp.int32, (BLK, BLK), 0)
    j = lax.broadcasted_iota(jnp.int32, (BLK, BLK), 1)
    base = jnp.exp(-jnp.abs(i - j).astype(F32) / TAPER_CELLS) * (1.0 / (members - 1))
    taper[0] = jnp.zeros((BLK, BLK), F32)
    for d in range(DISTS):
        taper[d + 1] = base * math.exp(-d / DIST_SCALE)
    col_blocks = col.shape[1] * group_rows
    for c in listed:
        c.wait()
    lists[...] = slot_lists(pairs[0], pairs[1], pairs[2], count[0, 0], col_blocks)
    to_smem = pltpu.make_async_copy(lists, list_smem, local_sem.at[3 * group_rows + 4])
    to_smem.start()

    for d in RING:
        for n in range(2):
            ev[n, d].wait_recv()
            along_second(n, -d)
            to_sib(n, -d, 0)
    @pl.when(z < NZ - 1)
    def _():
        pl.semaphore_wait(ready, NZ - 1 - z)

    for k in range(1, NZ):
        @pl.when(z + k < NZ)
        def _():
            zev[k - 1].start()

    for o in (0,) + RING:
        for e in RING:
            for n in range(2):
                ev[n, -o, e].wait_recv()
                to_sib(n, -o, -e)
    for c in zev:
        c.wait_recv()
    to_smem.wait()
    for c in sib_copies:
        c.wait_recv()

    tn = (((0,), (0,)), ((), ()))

    def entry(a, s):
        e = list_smem[0, a * SLOTS + s]
        q = e & (col_blocks - 1)
        return e // col_blocks, q // group_rows, q & (group_rows - 1)

    @pl.loop(0, NZ)
    def _(t):
        g = lax.rem(z + 1 + t, NZ)
        turns = SLOTS // GROUP
        steps = turns * group_rows
        products, tapered, sums = {}, {}, {}
        for i in range(steps + 2):
            if i < steps:
                b = i // turns
                xa = row[g, b]
                entries = [entry(g * group_rows + b, i % turns * GROUP + n) for n in range(GROUP)]
                products[i] = entries, [
                    lax.dot_general(col[0, q, k], xa, tn, preferred_element_type=F32) for _, q, k in entries
                ]
            if 1 <= i <= steps:
                entries, prods = products.pop(i - 1)
                tapered[i - 1] = entries, jnp.concatenate(
                    [(p * taper[d]).astype(BF16) for p, (d, _, _) in zip(prods, entries)], axis=0
                )
            if i >= 2:
                b, turn = divmod(i - 2, turns)
                entries, weights = tapered.pop(i - 2)
                vb = jnp.concatenate([col[1, q, k] for _, q, k in entries], axis=1)
                term = jnp.dot(vb, weights, preferred_element_type=F32)
                sums[b] = term if turn == 0 else sums[b] + term
                if turn == turns - 1:
                    done = sums.pop(b)
                    own[b] = done
                    part[t, b] = done.astype(BF16)

        @pl.when(t < NZ - 1)
        def _():
            pltpu.make_async_remote_copy(
                src_ref=part.at[t], dst_ref=landed.at[t], send_sem=rs_send.at[t], recv_sem=rs_recv.at[t],
                device_id=(r, g), device_id_type=MESH,
            ).start()

    total = own[...]
    for t in range(NZ - 1):
        done = pltpu.make_async_remote_copy(
            src_ref=part.at[t], dst_ref=landed.at[t], send_sem=rs_send.at[t], recv_sem=rs_recv.at[t],
            device_id=(r, lax.rem(z + 1, NZ)), device_id_type=MESH,
        )
        done.wait()
        total = total + landed[t].astype(F32)
    for b in range(group_rows):
        out_ref[:, b * BLK : (b + 1) * BLK] = total[b]
    for c in started:
        c.wait_send()


def local(anomalies, innovations, pair_rows, pair_cols, pair_dist, pair_counts):
    cells, members = anomalies.shape
    columns = innovations.shape[1]
    n_rows = lax.axis_size("rows")
    vm = pl.BlockSpec(memory_space=pltpu.VMEM)
    hbm = pl.BlockSpec(memory_space=pltpu.HBM)
    each = cells // BLK
    blocks = NZ * each
    out = pl.pallas_call(
        kernel,
        out_shape=jax.ShapeDtypeStruct((columns, cells), F32),
        in_specs=[hbm] * 6,
        out_specs=vm,
        scratch_shapes=[
            pltpu.SMEM(pair_counts.shape, jnp.int32),
            pltpu.VMEM((3,) + pair_rows.shape, jnp.int32),
            pltpu.VMEM((2, n_rows, each, members, BLK), BF16),
            pltpu.VMEM((NZ, each, members, BLK), BF16),
            pltpu.VMEM((DISTS + 1, BLK, BLK), F32),
            pltpu.VMEM((1, blocks * SLOTS), jnp.int32),
            pltpu.SMEM((1, blocks * SLOTS), jnp.int32),
            pltpu.VMEM((NZ, each, columns, BLK), BF16),
            pltpu.VMEM((each, columns, BLK), F32),
            pltpu.VMEM((NZ - 1, each, columns, BLK), BF16),
            pltpu.SemaphoreType.DMA((96,)),
            pltpu.SemaphoreType.DMA((96,)),
            pltpu.SemaphoreType.DMA((NZ - 1,)),
            pltpu.SemaphoreType.DMA((NZ - 1,)),
            pltpu.SemaphoreType.DMA((3 * each + 5,)),
            pltpu.SemaphoreType.REGULAR,
        ],
        compiler_params=pltpu.CompilerParams(
            collective_id=0, has_side_effects=True, vmem_limit_bytes=56 << 20
        ),
        name="increment",
    )(pair_counts, anomalies.T, innovations.T, pair_rows, pair_cols, pair_dist)
    return out.T


def solution(mesh):
    split = P(("rows", "cols"), None)
    pairs = P("rows", "cols")
    return jax.shard_map(
        local, mesh=mesh, in_specs=(split, split, pairs, pairs, pairs, pairs), out_specs=split, check_vma=False
    )
```

```python
import functools
import math

import jax
import jax.numpy as jnp
from jax import lax
from jax.experimental import pallas as pl
from jax.experimental.pallas import tpu as pltpu
from jax.sharding import PartitionSpec as P

BLK = 128
SLOTS = 32
GROUP = 8
TAPER_CELLS = 8
DIST_SCALE = 4.0
DISTS = 8
NY, NX, NZ = 4, 4, 8
MESH = pl.DeviceIdType.MESH
RING = (1, -1, 2)
F32, BF16 = jnp.float32, jnp.bfloat16


def slot_lists(rows, cols, dist, count, col_blocks):
    slots = rows.shape[1]
    chunks = range(slots // BLK)
    live = lax.broadcasted_iota(jnp.int32, (1, slots), 1) < count
    held = jnp.where(live, rows, 2 * slots)
    entry = (dist + 1) * col_blocks + cols
    lane = lax.broadcasted_iota(jnp.int32, (BLK, BLK), 1)
    earlier = lax.broadcasted_iota(jnp.int32, (BLK, BLK), 0) < lane

    def part(v, c):
        return v[:, c * BLK : (c + 1) * BLK]

    def down(v, c):
        return jnp.broadcast_to(part(v, c), (BLK, BLK)).T

    held_down = [down(held, c) for c in chunks]
    places = []
    for c in chunks:
        same = jnp.where((held_down[c] == part(held, c)) & earlier, 1, 0)
        for e in range(c):
            same = same + jnp.where(held_down[e] == part(held, c), 1, 0)
        places.append(part(held, c) * SLOTS + jnp.sum(same, axis=0, keepdims=True))
    place = jnp.concatenate(places, axis=1)
    place_down = [down(place, c) for c in chunks]
    entry_down = [down(entry, c) for c in chunks]
    out = []
    for c in chunks:
        found = jnp.zeros((BLK, BLK), jnp.int32)
        for e in chunks:
            found = found + jnp.where(place_down[e] == lane + c * BLK, entry_down[e], 0)
        out.append(jnp.sum(found, axis=0, keepdims=True))
    return jnp.concatenate(out, axis=1)


def kernel(
    count_ref, x_ref, v_ref, rows_ref, cols_ref, dist_ref, out_ref,
    count, pairs, col, row, taper, lists, list_smem, part, own, landed,
    send_sem, recv_sem, rs_send, rs_recv, local_sem, ready,
):
    r, z = lax.axis_index("rows"), lax.axis_index("cols")
    core = lax.rem(r, 2)
    chip = r // 2
    x, y = lax.rem(chip, NX), chip // NX
    members, cells = x_ref.shape

    def dev(yy, xx):
        return (lax.rem(yy + NY, NY) * NX + lax.rem(xx + NX, NX)) * 2 + core

    sib = r + 1 - 2 * core

    group_rows = cells // BLK
    mine = []
    for n, (src, dst) in enumerate(((x_ref, col.at[0, r]), (v_ref, col.at[1, r]), (x_ref, row.at[z]))):
        for b in range(group_rows):
            mine.append(
                pltpu.make_async_copy(
                    src.at[:, b * BLK : (b + 1) * BLK], dst.at[b], local_sem.at[n * group_rows + b]
                )
            )
    for c in mine:
        c.start()
    listed = [pltpu.make_async_copy(count_ref, count, local_sem.at[3 * group_rows])]
    for n, ref in enumerate((rows_ref, cols_ref, dist_ref)):
        listed.append(pltpu.make_async_copy(ref, pairs.at[n], local_sem.at[3 * group_rows + 1 + n]))
    for c in listed:
        c.start()

    barrier = pltpu.get_barrier_semaphore()
    peers = [(sib, z)]
    peers += [(dev(y, x + d), z) for d in RING] + [(dev(y + d, x), z) for d in RING]
    for peer in peers:
        pl.semaphore_signal(barrier, inc=1, device_id=peer, device_id_type=MESH)
    for k in range(1, NZ):
        @pl.when(z + k < NZ)
        def _():
            pl.semaphore_signal(barrier, inc=1, device_id=(r, lax.rem(z + k, NZ)), device_id_type=MESH)

    for c in mine:
        c.wait()
    pl.semaphore_wait(barrier, len(peers) + z)
    for k in range(1, NZ):
        @pl.when(z + k >= NZ)
        def _():
            pl.semaphore_signal(ready, inc=1, device_id=(r, lax.rem(z + k, NZ)), device_id_type=MESH)

    started = []

    def copy(src, device, k):
        c = pltpu.make_async_remote_copy(
            src_ref=src, dst_ref=src, send_sem=send_sem.at[k], recv_sem=recv_sem.at[k],
            device_id=device, device_id_type=MESH,
        )
        started.append(c)
        return c

    def push(src, device, k):
        c = copy(src, device, k)
        c.start()
        return c

    counter = iter(range(1000))

    def key():
        return next(counter)

    def place(n, o, e):
        return dev(y + (o if n else e), x + (e if n else o))

    def slab(n, o, e):
        return col.at[n, place(n, o, e)]

    ev = {}
    sib_copies = []

    def to_sib(n, o, e):
        sib_copies.append(push(slab(n, o, e), (sib, z), key()))

    def along_second(n, o):
        for e in RING:
            ev[n, o, e] = push(slab(n, o, 0), (place(n, 0, e), z), key())

    for d in RING:
        for n in range(2):
            ev[n, d] = push(slab(n, 0, 0), (place(n, d, 0), z), key())
    for n in range(2):
        along_second(n, 0)
    zev = [copy(row.at[z], (r, lax.rem(z + k, NZ)), key()) for k in range(1, NZ)]
    for k in range(1, NZ):
        @pl.when(z + k >= NZ)
        def _():
            zev[k - 1].start()

    for n in range(2):
        to_sib(n, 0, 0)

    i = lax.broadcasted_iota(jnp.int32, (BLK, BLK), 0)
    j = lax.broadcasted_iota(jnp.int32, (BLK, BLK), 1)
    base = jnp.exp(-jnp.abs(i - j).astype(F32) / TAPER_CELLS) * (1.0 / (members - 1))
    taper[0] = jnp.zeros((BLK, BLK), F32)
    for d in range(DISTS):
        taper[d + 1] = base * math.exp(-d / DIST_SCALE)
    col_blocks = col.shape[1] * group_rows
    for c in listed:
        c.wait()
    lists[...] = slot_lists(pairs[0], pairs[1], pairs[2], count[0, 0], col_blocks)
    to_smem = pltpu.make_async_copy(lists, list_smem, local_sem.at[3 * group_rows + 4])
    to_smem.start()

    for d in RING:
        for n in range(2):
            ev[n, d].wait_recv()
            along_second(n, -d)
            to_sib(n, -d, 0)
    @pl.when(z < NZ - 1)
    def _():
        pl.semaphore_wait(ready, NZ - 1 - z)

    for k in range(1, NZ):
        @pl.when(z + k < NZ)
        def _():
            zev[k - 1].start()

    for o in (0,) + RING:
        for e in RING:
            for n in range(2):
                ev[n, -o, e].wait_recv()
                to_sib(n, -o, -e)
    for c in zev:
        c.wait_recv()
    to_smem.wait()
    for c in sib_copies:
        c.wait_recv()

    tn = (((0,), (0,)), ((), ()))

    def entry(a, s):
        e = list_smem[0, a * SLOTS + s]
        q = e & (col_blocks - 1)
        return e // col_blocks, q // group_rows, q & (group_rows - 1)

    def target(t):
        half = NZ // 2
        low = z // half * half
        sign = 1 - 2 * lax.rem(z, 2)
        across = (half - low) + lax.rem(z + sign * t + half, half)
        near = low + lax.rem(z + t + 1, half)
        return jnp.where(t < half, across, near)

    @pl.loop(0, NZ)
    def _(t):
        g = target(t)
        turns = SLOTS // GROUP
        steps = turns * group_rows
        products, tapered, sums = {}, {}, {}
        for i in range(steps + 2):
            if i < steps:
                b = i // turns
                xa = row[g, b]
                entries = [entry(g * group_rows + b, i % turns * GROUP + n) for n in range(GROUP)]
                products[i] = entries, [
                    lax.dot_general(col[0, q, k], xa, tn, preferred_element_type=F32) for _, q, k in entries
                ]
            if 1 <= i <= steps:
                entries, prods = products.pop(i - 1)
                tapered[i - 1] = entries, jnp.concatenate(
                    [(p * taper[d]).astype(BF16) for p, (d, _, _) in zip(prods, entries)], axis=0
                )
            if i >= 2:
                b, turn = divmod(i - 2, turns)
                entries, weights = tapered.pop(i - 2)
                vb = jnp.concatenate([col[1, q, k] for _, q, k in entries], axis=1)
                term = jnp.dot(vb, weights, preferred_element_type=F32)
                sums[b] = term if turn == 0 else sums[b] + term
                if turn == turns - 1:
                    done = sums.pop(b)
                    own[b] = done
                    part[t, b] = done.astype(BF16)

        @pl.when(t < NZ - 1)
        def _():
            pltpu.make_async_remote_copy(
                src_ref=part.at[t], dst_ref=landed.at[z], send_sem=rs_send.at[t], recv_sem=rs_recv.at[z],
                device_id=(r, g), device_id_type=MESH,
            ).start()

    total = own[...]
    for k in range(1, NZ):
        source = lax.rem(z + k, NZ)
        done = pltpu.make_async_remote_copy(
            src_ref=part.at[k - 1], dst_ref=landed.at[source], send_sem=rs_send.at[k - 1],
            recv_sem=rs_recv.at[source], device_id=(r, source), device_id_type=MESH,
        )
        done.wait()
        total = total + landed[source].astype(F32)
    for b in range(group_rows):
        out_ref[:, b * BLK : (b + 1) * BLK] = total[b]
    for c in started:
        c.wait_send()


def local(anomalies, innovations, pair_rows, pair_cols, pair_dist, pair_counts):
    cells, members = anomalies.shape
    columns = innovations.shape[1]
    n_rows = lax.axis_size("rows")
    vm = pl.BlockSpec(memory_space=pltpu.VMEM)
    hbm = pl.BlockSpec(memory_space=pltpu.HBM)
    each = cells // BLK
    blocks = NZ * each
    out = pl.pallas_call(
        kernel,
        out_shape=jax.ShapeDtypeStruct((columns, cells), F32),
        in_specs=[hbm] * 6,
        out_specs=vm,
        scratch_shapes=[
            pltpu.SMEM(pair_counts.shape, jnp.int32),
            pltpu.VMEM((3,) + pair_rows.shape, jnp.int32),
            pltpu.VMEM((2, n_rows, each, members, BLK), BF16),
            pltpu.VMEM((NZ, each, members, BLK), BF16),
            pltpu.VMEM((DISTS + 1, BLK, BLK), F32),
            pltpu.VMEM((1, blocks * SLOTS), jnp.int32),
            pltpu.SMEM((1, blocks * SLOTS), jnp.int32),
            pltpu.VMEM((NZ, each, columns, BLK), BF16),
            pltpu.VMEM((each, columns, BLK), F32),
            pltpu.VMEM((NZ, each, columns, BLK), BF16),
            pltpu.SemaphoreType.DMA((96,)),
            pltpu.SemaphoreType.DMA((96,)),
            pltpu.SemaphoreType.DMA((NZ - 1,)),
            pltpu.SemaphoreType.DMA((NZ,)),
            pltpu.SemaphoreType.DMA((3 * each + 5,)),
            pltpu.SemaphoreType.REGULAR,
        ],
        compiler_params=pltpu.CompilerParams(
            collective_id=0, has_side_effects=True, vmem_limit_bytes=56 << 20
        ),
        name="increment",
    )(pair_counts, anomalies.T, innovations.T, pair_rows, pair_cols, pair_dist)
    return out.T


def solution(mesh):
    split = P(("rows", "cols"), None)
    pairs = P("rows", "cols")
    return jax.shard_map(
        local, mesh=mesh, in_specs=(split, split, pairs, pairs, pairs, pairs), out_specs=split, check_vma=False
    )
```

```python
import functools
import math

import jax
import jax.numpy as jnp
from jax import lax
from jax.experimental import pallas as pl
from jax.experimental.pallas import tpu as pltpu
from jax.sharding import PartitionSpec as P

BLK = 128
SLOTS = 32
GROUP = 8
TAPER_CELLS = 8
DIST_SCALE = 4.0
DISTS = 8
NY, NX, NZ = 4, 4, 8
MESH = pl.DeviceIdType.MESH
RING = (1, -1, 2)
F32, BF16 = jnp.float32, jnp.bfloat16


def slot_lists(rows, cols, dist, count, col_blocks):
    slots = rows.shape[1]
    chunks = range(slots // BLK)
    live = lax.broadcasted_iota(jnp.int32, (1, slots), 1) < count
    held = jnp.where(live, rows, 2 * slots)
    entry = (dist + 1) * col_blocks + cols
    lane = lax.broadcasted_iota(jnp.int32, (BLK, BLK), 1)
    earlier = lax.broadcasted_iota(jnp.int32, (BLK, BLK), 0) < lane

    def part(v, c):
        return v[:, c * BLK : (c + 1) * BLK]

    def down(v, c):
        return jnp.broadcast_to(part(v, c), (BLK, BLK)).T

    held_down = [down(held, c) for c in chunks]
    places = []
    for c in chunks:
        same = jnp.where((held_down[c] == part(held, c)) & earlier, 1, 0)
        for e in range(c):
            same = same + jnp.where(held_down[e] == part(held, c), 1, 0)
        places.append(part(held, c) * SLOTS + jnp.sum(same, axis=0, keepdims=True))
    place = jnp.concatenate(places, axis=1)
    place_down = [down(place, c) for c in chunks]
    entry_down = [down(entry, c) for c in chunks]
    out = []
    for c in chunks:
        found = jnp.zeros((BLK, BLK), jnp.int32)
        for e in chunks:
            found = found + jnp.where(place_down[e] == lane + c * BLK, entry_down[e], 0)
        out.append(jnp.sum(found, axis=0, keepdims=True))
    return jnp.concatenate(out, axis=1)


def kernel(
    count_ref, x_ref, v_ref, rows_ref, cols_ref, dist_ref, out_ref,
    count, pairs, col, row, taper, lists, list_smem, part, own, landed,
    send_sem, recv_sem, rs_send, rs_recv, local_sem, ready,
):
    r, z = lax.axis_index("rows"), lax.axis_index("cols")
    core = lax.rem(r, 2)
    chip = r // 2
    x, y = lax.rem(chip, NX), chip // NX
    members, cells = x_ref.shape

    def dev(yy, xx):
        return (lax.rem(yy + NY, NY) * NX + lax.rem(xx + NX, NX)) * 2 + core

    sib = r + 1 - 2 * core

    group_rows = cells // BLK
    mine = []
    for n, (src, dst) in enumerate(((x_ref, col.at[0, r]), (v_ref, col.at[1, r]), (x_ref, row.at[z]))):
        for b in range(group_rows):
            mine.append(
                pltpu.make_async_copy(
                    src.at[:, b * BLK : (b + 1) * BLK], dst.at[b], local_sem.at[n * group_rows + b]
                )
            )
    for c in mine:
        c.start()
    listed = [pltpu.make_async_copy(count_ref, count, local_sem.at[3 * group_rows])]
    for n, ref in enumerate((rows_ref, cols_ref, dist_ref)):
        listed.append(pltpu.make_async_copy(ref, pairs.at[n], local_sem.at[3 * group_rows + 1 + n]))
    for c in listed:
        c.start()

    barrier = pltpu.get_barrier_semaphore()
    peers = [(sib, z)]
    peers += [(dev(y, x + d), z) for d in RING] + [(dev(y + d, x), z) for d in RING]
    for peer in peers:
        pl.semaphore_signal(barrier, inc=1, device_id=peer, device_id_type=MESH)
    for k in range(1, NZ):
        @pl.when(z + k < NZ)
        def _():
            pl.semaphore_signal(barrier, inc=1, device_id=(r, lax.rem(z + k, NZ)), device_id_type=MESH)

    for c in mine:
        c.wait()
    pl.semaphore_wait(barrier, len(peers) + z)
    for k in range(1, NZ):
        @pl.when(z + k >= NZ)
        def _():
            pl.semaphore_signal(ready, inc=1, device_id=(r, lax.rem(z + k, NZ)), device_id_type=MESH)

    started = []

    def copy(src, device, k):
        c = pltpu.make_async_remote_copy(
            src_ref=src, dst_ref=src, send_sem=send_sem.at[k], recv_sem=recv_sem.at[k],
            device_id=device, device_id_type=MESH,
        )
        started.append(c)
        return c

    def push(src, device, k):
        c = copy(src, device, k)
        c.start()
        return c

    counter = iter(range(1000))

    def key():
        return next(counter)

    def place(n, o, e):
        return dev(y + (o if n else e), x + (e if n else o))

    def slab(n, o, e):
        return col.at[n, place(n, o, e)]

    ev = {}
    sib_copies = []

    def to_sib(n, o, e):
        sib_copies.append(push(slab(n, o, e), (sib, z), key()))

    def along_second(n, o):
        for e in RING:
            ev[n, o, e] = push(slab(n, o, 0), (place(n, 0, e), z), key())

    for d in RING:
        for n in range(2):
            ev[n, d] = push(slab(n, 0, 0), (place(n, d, 0), z), key())
    for n in range(2):
        along_second(n, 0)
    zev = [copy(row.at[z], (r, lax.rem(z + k, NZ)), key()) for k in range(1, NZ)]
    for k in range(1, NZ):
        @pl.when(z + k >= NZ)
        def _():
            zev[k - 1].start()

    for n in range(2):
        to_sib(n, 0, 0)

    i = lax.broadcasted_iota(jnp.int32, (BLK, BLK), 0)
    j = lax.broadcasted_iota(jnp.int32, (BLK, BLK), 1)
    base = jnp.exp(-jnp.abs(i - j).astype(F32) / TAPER_CELLS) * (1.0 / (members - 1))
    taper[0] = jnp.zeros((BLK, BLK), F32)
    for d in range(DISTS):
        taper[d + 1] = base * math.exp(-d / DIST_SCALE)
    col_blocks = col.shape[1] * group_rows
    for c in listed:
        c.wait()
    lists[...] = slot_lists(pairs[0], pairs[1], pairs[2], count[0, 0], col_blocks)
    to_smem = pltpu.make_async_copy(lists, list_smem, local_sem.at[3 * group_rows + 4])
    to_smem.start()

    for d in RING:
        for n in range(2):
            ev[n, d].wait_recv()
            along_second(n, -d)
            to_sib(n, -d, 0)
    @pl.when(z < NZ - 1)
    def _():
        pl.semaphore_wait(ready, NZ - 1 - z)

    for k in range(1, NZ):
        @pl.when(z + k < NZ)
        def _():
            zev[k - 1].start()

    for o in (0,) + RING:
        for e in RING:
            for n in range(2):
                ev[n, -o, e].wait_recv()
                to_sib(n, -o, -e)
    for c in zev:
        c.wait_recv()
    to_smem.wait()
    for c in sib_copies:
        c.wait_recv()

    tn = (((0,), (0,)), ((), ()))

    def entry(a, s):
        e = list_smem[0, a * SLOTS + s]
        q = e & (col_blocks - 1)
        return e // col_blocks, q // group_rows, q & (group_rows - 1)

    def target(t):
        half = NZ // 2
        low = z // half * half
        across = (half - low) + t + lax.rem(z, 2) * (1 - 2 * lax.rem(t, 2))
        near = low + lax.rem(z + t + 1, half)
        return jnp.where(t < half, across, near)

    @pl.loop(0, NZ)
    def _(t):
        g = target(t)
        turns = SLOTS // GROUP
        steps = turns * group_rows
        products, tapered, sums = {}, {}, {}
        for i in range(steps + 2):
            if i < steps:
                b = i // turns
                xa = row[g, b]
                entries = [entry(g * group_rows + b, i % turns * GROUP + n) for n in range(GROUP)]
                products[i] = entries, [
                    lax.dot_general(col[0, q, k], xa, tn, preferred_element_type=F32) for _, q, k in entries
                ]
            if 1 <= i <= steps:
                entries, prods = products.pop(i - 1)
                tapered[i - 1] = entries, jnp.concatenate(
                    [(p * taper[d]).astype(BF16) for p, (d, _, _) in zip(prods, entries)], axis=0
                )
            if i >= 2:
                b, turn = divmod(i - 2, turns)
                entries, weights = tapered.pop(i - 2)
                vb = jnp.concatenate([col[1, q, k] for _, q, k in entries], axis=1)
                term = jnp.dot(vb, weights, preferred_element_type=F32)
                sums[b] = term if turn == 0 else sums[b] + term
                if turn == turns - 1:
                    done = sums.pop(b)
                    own[b] = done
                    part[t, b] = done.astype(BF16)

        @pl.when(t < NZ - 1)
        def _():
            pltpu.make_async_remote_copy(
                src_ref=part.at[t], dst_ref=landed.at[z], send_sem=rs_send.at[t], recv_sem=rs_recv.at[z],
                device_id=(r, g), device_id_type=MESH,
            ).start()

    total = own[...]
    for k in range(1, NZ):
        source = lax.rem(z + k, NZ)
        done = pltpu.make_async_remote_copy(
            src_ref=part.at[k - 1], dst_ref=landed.at[source], send_sem=rs_send.at[k - 1],
            recv_sem=rs_recv.at[source], device_id=(r, source), device_id_type=MESH,
        )
        done.wait()
        total = total + landed[source].astype(F32)
    for b in range(group_rows):
        out_ref[:, b * BLK : (b + 1) * BLK] = total[b]
    for c in started:
        c.wait_send()


def local(anomalies, innovations, pair_rows, pair_cols, pair_dist, pair_counts):
    cells, members = anomalies.shape
    columns = innovations.shape[1]
    n_rows = lax.axis_size("rows")
    vm = pl.BlockSpec(memory_space=pltpu.VMEM)
    hbm = pl.BlockSpec(memory_space=pltpu.HBM)
    each = cells // BLK
    blocks = NZ * each
    out = pl.pallas_call(
        kernel,
        out_shape=jax.ShapeDtypeStruct((columns, cells), F32),
        in_specs=[hbm] * 6,
        out_specs=vm,
        scratch_shapes=[
            pltpu.SMEM(pair_counts.shape, jnp.int32),
            pltpu.VMEM((3,) + pair_rows.shape, jnp.int32),
            pltpu.VMEM((2, n_rows, each, members, BLK), BF16),
            pltpu.VMEM((NZ, each, members, BLK), BF16),
            pltpu.VMEM((DISTS + 1, BLK, BLK), F32),
            pltpu.VMEM((1, blocks * SLOTS), jnp.int32),
            pltpu.SMEM((1, blocks * SLOTS), jnp.int32),
            pltpu.VMEM((NZ, each, columns, BLK), BF16),
            pltpu.VMEM((each, columns, BLK), F32),
            pltpu.VMEM((NZ, each, columns, BLK), BF16),
            pltpu.SemaphoreType.DMA((96,)),
            pltpu.SemaphoreType.DMA((96,)),
            pltpu.SemaphoreType.DMA((NZ - 1,)),
            pltpu.SemaphoreType.DMA((NZ,)),
            pltpu.SemaphoreType.DMA((3 * each + 5,)),
            pltpu.SemaphoreType.REGULAR,
        ],
        compiler_params=pltpu.CompilerParams(
            collective_id=0, has_side_effects=True, vmem_limit_bytes=56 << 20
        ),
        name="increment",
    )(pair_counts, anomalies.T, innovations.T, pair_rows, pair_cols, pair_dist)
    return out.T


def solution(mesh):
    split = P(("rows", "cols"), None)
    pairs = P("rows", "cols")
    return jax.shard_map(
        local, mesh=mesh, in_specs=(split, split, pairs, pairs, pairs, pairs), out_specs=split, check_vma=False
    )
```

```python
import functools
import math

import jax
import jax.numpy as jnp
from jax import lax
from jax.experimental import pallas as pl
from jax.experimental.pallas import tpu as pltpu
from jax.sharding import PartitionSpec as P

BLK = 128
SLOTS = 32
GROUP = 8
TAPER_CELLS = 8
DIST_SCALE = 4.0
DISTS = 8
NY, NX, NZ = 4, 4, 8
MESH = pl.DeviceIdType.MESH
RING = (1, -1, 2)
F32, BF16 = jnp.float32, jnp.bfloat16


def slot_lists(rows, cols, dist, count, col_blocks):
    slots = rows.shape[1]
    chunks = range(slots // BLK)
    live = lax.broadcasted_iota(jnp.int32, (1, slots), 1) < count
    held = jnp.where(live, rows, 2 * slots)
    entry = (dist + 1) * col_blocks + cols
    lane = lax.broadcasted_iota(jnp.int32, (BLK, BLK), 1)
    earlier = lax.broadcasted_iota(jnp.int32, (BLK, BLK), 0) < lane

    def part(v, c):
        return v[:, c * BLK : (c + 1) * BLK]

    def down(v, c):
        return jnp.broadcast_to(part(v, c), (BLK, BLK)).T

    held_down = [down(held, c) for c in chunks]
    places = []
    for c in chunks:
        same = jnp.where((held_down[c] == part(held, c)) & earlier, 1, 0)
        for e in range(c):
            same = same + jnp.where(held_down[e] == part(held, c), 1, 0)
        places.append(part(held, c) * SLOTS + jnp.sum(same, axis=0, keepdims=True))
    place = jnp.concatenate(places, axis=1)
    place_down = [down(place, c) for c in chunks]
    entry_down = [down(entry, c) for c in chunks]
    out = []
    for c in chunks:
        found = jnp.zeros((BLK, BLK), jnp.int32)
        for e in chunks:
            found = found + jnp.where(place_down[e] == lane + c * BLK, entry_down[e], 0)
        out.append(jnp.sum(found, axis=0, keepdims=True))
    return jnp.concatenate(out, axis=1)


def kernel(
    count_ref, x_ref, v_ref, rows_ref, cols_ref, dist_ref, out_ref,
    count, pairs, col, row, taper, lists, list_smem, part, own, landed,
    send_sem, recv_sem, rs_send, rs_recv, local_sem, ready,
):
    r, z = lax.axis_index("rows"), lax.axis_index("cols")
    core = lax.rem(r, 2)
    chip = r // 2
    x, y = lax.rem(chip, NX), chip // NX
    members, cells = x_ref.shape

    def dev(yy, xx):
        return (lax.rem(yy + NY, NY) * NX + lax.rem(xx + NX, NX)) * 2 + core

    sib = r + 1 - 2 * core

    group_rows = cells // BLK
    mine = []
    for n, (src, dst) in enumerate(((x_ref, col.at[0, r]), (v_ref, col.at[1, r]), (x_ref, row.at[z]))):
        for b in range(group_rows):
            mine.append(
                pltpu.make_async_copy(
                    src.at[:, b * BLK : (b + 1) * BLK], dst.at[b], local_sem.at[n * group_rows + b]
                )
            )
    for c in mine:
        c.start()
    listed = [pltpu.make_async_copy(count_ref, count, local_sem.at[3 * group_rows])]
    for n, ref in enumerate((rows_ref, cols_ref, dist_ref)):
        listed.append(pltpu.make_async_copy(ref, pairs.at[n], local_sem.at[3 * group_rows + 1 + n]))
    for c in listed:
        c.start()

    barrier = pltpu.get_barrier_semaphore()
    peers = [(sib, z)]
    peers += [(dev(y, x + d), z) for d in RING] + [(dev(y + d, x), z) for d in RING]
    for peer in peers:
        pl.semaphore_signal(barrier, inc=1, device_id=peer, device_id_type=MESH)
    for k in range(1, NZ):
        @pl.when(z + k < NZ)
        def _():
            pl.semaphore_signal(barrier, inc=1, device_id=(r, lax.rem(z + k, NZ)), device_id_type=MESH)

    for c in mine:
        c.wait()
    pl.semaphore_wait(barrier, len(peers) + z)
    for k in range(1, NZ):
        @pl.when(z + k >= NZ)
        def _():
            pl.semaphore_signal(ready, inc=1, device_id=(r, lax.rem(z + k, NZ)), device_id_type=MESH)

    started = []

    def copy(src, device, k):
        c = pltpu.make_async_remote_copy(
            src_ref=src, dst_ref=src, send_sem=send_sem.at[k], recv_sem=recv_sem.at[k],
            device_id=device, device_id_type=MESH,
        )
        started.append(c)
        return c

    def push(src, device, k):
        c = copy(src, device, k)
        c.start()
        return c

    counter = iter(range(1000))

    def key():
        return next(counter)

    def place(n, o, e):
        return dev(y + (o if n else e), x + (e if n else o))

    def slab(n, o, e):
        return col.at[n, place(n, o, e)]

    ev = {}
    sib_copies = []

    def to_sib(n, o, e):
        sib_copies.append(push(slab(n, o, e), (sib, z), key()))

    def along_second(n, o):
        for e in RING:
            ev[n, o, e] = push(slab(n, o, 0), (place(n, 0, e), z), key())

    for d in RING:
        for n in range(2):
            ev[n, d] = push(slab(n, 0, 0), (place(n, d, 0), z), key())
    for n in range(2):
        along_second(n, 0)
    zev = [copy(row.at[z], (r, lax.rem(z + k, NZ)), key()) for k in range(1, NZ)]
    for k in range(1, NZ):
        @pl.when(z + k >= NZ)
        def _():
            zev[k - 1].start()

    for n in range(2):
        to_sib(n, 0, 0)

    i = lax.broadcasted_iota(jnp.int32, (BLK, BLK), 0)
    j = lax.broadcasted_iota(jnp.int32, (BLK, BLK), 1)
    base = jnp.exp(-jnp.abs(i - j).astype(F32) / TAPER_CELLS) * (1.0 / (members - 1))
    taper[0] = jnp.zeros((BLK, BLK), F32)
    for d in range(DISTS):
        taper[d + 1] = base * math.exp(-d / DIST_SCALE)
    col_blocks = col.shape[1] * group_rows
    for c in listed:
        c.wait()
    lists[...] = slot_lists(pairs[0], pairs[1], pairs[2], count[0, 0], col_blocks)
    to_smem = pltpu.make_async_copy(lists, list_smem, local_sem.at[3 * group_rows + 4])
    to_smem.start()

    for d in RING:
        for n in range(2):
            ev[n, d].wait_recv()
            along_second(n, -d)
            to_sib(n, -d, 0)
    @pl.when(z < NZ - 1)
    def _():
        pl.semaphore_wait(ready, NZ - 1 - z)

    for k in range(1, NZ):
        @pl.when(z + k < NZ)
        def _():
            zev[k - 1].start()

    for o in (0,) + RING:
        for e in RING:
            for n in range(2):
                ev[n, -o, e].wait_recv()
                to_sib(n, -o, -e)
    for c in zev:
        c.wait_recv()
    to_smem.wait()
    for c in sib_copies:
        c.wait_recv()

    tn = (((0,), (0,)), ((), ()))

    def entry(a, s):
        e = list_smem[0, a * SLOTS + s]
        q = e & (col_blocks - 1)
        return e // col_blocks, q // group_rows, q & (group_rows - 1)

    def target(t):
        half = NZ // 2
        low = z // half * half
        across = (half - low) + t + lax.rem(z, 2) * (1 - 2 * lax.rem(t, 2))
        near = low + lax.rem(z + t + 1, half)
        return jnp.where(t < half, across, near)

    @pl.loop(0, NZ)
    def _(t):
        g = target(t)
        turns = SLOTS // GROUP
        steps = turns * group_rows
        products, tapered, sums = {}, {}, {}
        for i in range(steps + 2):
            if i < steps:
                b = i // turns
                xa = row[g, b]
                entries = [entry(g * group_rows + b, i % turns * GROUP + n) for n in range(GROUP)]
                products[i] = entries, [
                    lax.dot_general(col[0, q, k], xa, tn, preferred_element_type=F32) for _, q, k in entries
                ]
            if 1 <= i <= steps:
                entries, prods = products.pop(i - 1)
                tapered[i - 1] = entries, jnp.concatenate(
                    [(p * taper[d]).astype(BF16) for p, (d, _, _) in zip(prods, entries)], axis=0
                )
            if i >= 2:
                b, turn = divmod(i - 2, turns)
                entries, weights = tapered.pop(i - 2)
                vb = jnp.concatenate([col[1, q, k] for _, q, k in entries], axis=1)
                term = jnp.dot(vb, weights, preferred_element_type=F32)
                sums[b] = term if turn == 0 else sums[b] + term
                if turn == turns - 1:
                    done = sums.pop(b)
                    own[b] = done
                    part[t, b] = done.astype(BF16)

        @pl.when(t < NZ - 1)
        def _():
            pltpu.make_async_remote_copy(
                src_ref=part.at[t], dst_ref=landed.at[z], send_sem=rs_send.at[t], recv_sem=rs_recv.at[z],
                device_id=(r, g), device_id_type=MESH,
            ).start()

    total = own[...]
    for k in range(1, NZ):
        source = lax.rem(z + k, NZ)
        done = pltpu.make_async_remote_copy(
            src_ref=part.at[k - 1], dst_ref=landed.at[source], send_sem=rs_send.at[k - 1],
            recv_sem=rs_recv.at[source], device_id=(r, source), device_id_type=MESH,
        )
        done.wait()
        total = total + landed[source].astype(F32)
    for b in range(group_rows):
        out_ref[:, b * BLK : (b + 1) * BLK] = total[b]
    for c in started:
        c.wait_send()


def local(anomalies, innovations, pair_rows, pair_cols, pair_dist, pair_counts):
    cells, members = anomalies.shape
    columns = innovations.shape[1]
    n_rows = lax.axis_size("rows")
    vm = pl.BlockSpec(memory_space=pltpu.VMEM)
    hbm = pl.BlockSpec(memory_space=pltpu.HBM)
    each = cells // BLK
    blocks = NZ * each
    operands = anomalies.T, innovations.T, pair_rows, pair_cols, pair_dist
    out = pl.pallas_call(
        kernel,
        out_shape=jax.ShapeDtypeStruct((columns, cells), F32),
        in_specs=[hbm] * 6,
        out_specs=vm,
        scratch_shapes=[
            pltpu.SMEM(pair_counts.shape, jnp.int32),
            pltpu.VMEM((3,) + pair_rows.shape, jnp.int32),
            pltpu.VMEM((2, n_rows, each, members, BLK), BF16),
            pltpu.VMEM((NZ, each, members, BLK), BF16),
            pltpu.VMEM((DISTS + 1, BLK, BLK), F32),
            pltpu.VMEM((1, blocks * SLOTS), jnp.int32),
            pltpu.SMEM((1, blocks * SLOTS), jnp.int32),
            pltpu.VMEM((NZ, each, columns, BLK), BF16),
            pltpu.VMEM((each, columns, BLK), F32),
            pltpu.VMEM((NZ, each, columns, BLK), BF16),
            pltpu.SemaphoreType.DMA((96,)),
            pltpu.SemaphoreType.DMA((96,)),
            pltpu.SemaphoreType.DMA((NZ - 1,)),
            pltpu.SemaphoreType.DMA((NZ,)),
            pltpu.SemaphoreType.DMA((3 * each + 5,)),
            pltpu.SemaphoreType.REGULAR,
        ],
        compiler_params=pltpu.CompilerParams(
            collective_id=0, has_side_effects=True, vmem_limit_bytes=40 << 20
        ),
        name="increment",
    )(pair_counts, *(pltpu.with_memory_space_constraint(o, pltpu.HBM) for o in operands))
    return out.T


def solution(mesh):
    split = P(("rows", "cols"), None)
    pairs = P("rows", "cols")
    return jax.shard_map(
        local, mesh=mesh, in_specs=(split, split, pairs, pairs, pairs, pairs), out_specs=split, check_vma=False
    )
```

```python
import functools
import math

import jax
import jax.numpy as jnp
from jax import lax
from jax.experimental import pallas as pl
from jax.experimental.pallas import tpu as pltpu
from jax.sharding import PartitionSpec as P

BLK = 128
SLOTS = 32
GROUP = 8
TAPER_CELLS = 8
DIST_SCALE = 4.0
DISTS = 8
NY, NX, NZ = 4, 4, 8
MESH = pl.DeviceIdType.MESH
RING = (1, -1, 2)
F32, BF16 = jnp.float32, jnp.bfloat16


def slot_lists(rows, cols, dist, count, col_blocks):
    slots = rows.shape[1]
    chunks = range(slots // BLK)
    live = lax.broadcasted_iota(jnp.int32, (1, slots), 1) < count
    held = jnp.where(live, rows, 2 * slots)
    entry = (dist + 1) * col_blocks + cols
    lane = lax.broadcasted_iota(jnp.int32, (BLK, BLK), 1)
    earlier = lax.broadcasted_iota(jnp.int32, (BLK, BLK), 0) < lane

    def part(v, c):
        return v[:, c * BLK : (c + 1) * BLK]

    def down(v, c):
        return jnp.broadcast_to(part(v, c), (BLK, BLK)).T

    held_down = [down(held, c) for c in chunks]
    places = []
    for c in chunks:
        same = jnp.where((held_down[c] == part(held, c)) & earlier, 1, 0)
        for e in range(c):
            same = same + jnp.where(held_down[e] == part(held, c), 1, 0)
        places.append(part(held, c) * SLOTS + jnp.sum(same, axis=0, keepdims=True))
    place = jnp.concatenate(places, axis=1)
    place_down = [down(place, c) for c in chunks]
    entry_down = [down(entry, c) for c in chunks]
    out = []
    for c in chunks:
        found = jnp.zeros((BLK, BLK), jnp.int32)
        for e in chunks:
            found = found + jnp.where(place_down[e] == lane + c * BLK, entry_down[e], 0)
        out.append(jnp.sum(found, axis=0, keepdims=True))
    return jnp.concatenate(out, axis=1)


def kernel(
    count_ref, x_ref, v_ref, rows_ref, cols_ref, dist_ref, out_ref,
    count, pairs, col, row, taper, lists, list_smem, part, own, landed,
    send_sem, recv_sem, rs_send, rs_recv, local_sem, ready,
):
    r, z = lax.axis_index("rows"), lax.axis_index("cols")
    core = lax.rem(r, 2)
    chip = r // 2
    x, y = lax.rem(chip, NX), chip // NX
    members, cells = x_ref.shape

    def dev(yy, xx):
        return (lax.rem(yy + NY, NY) * NX + lax.rem(xx + NX, NX)) * 2 + core

    sib = r + 1 - 2 * core

    group_rows = cells // BLK
    mine = []
    own_blocks = pl.ds(r * group_rows, group_rows)
    copies_in = ((x_ref, col.at[0, own_blocks]), (v_ref, col.at[1, own_blocks]), (x_ref, row.at[z]))
    for n, (src, dst) in enumerate(copies_in):
        for b in range(group_rows):
            mine.append(
                pltpu.make_async_copy(
                    src.at[:, b * BLK : (b + 1) * BLK], dst.at[b], local_sem.at[n * group_rows + b]
                )
            )
    for c in mine:
        c.start()
    listed = [pltpu.make_async_copy(count_ref, count, local_sem.at[3 * group_rows])]
    for n, ref in enumerate((rows_ref, cols_ref, dist_ref)):
        listed.append(pltpu.make_async_copy(ref, pairs.at[n], local_sem.at[3 * group_rows + 1 + n]))
    for c in listed:
        c.start()

    barrier = pltpu.get_barrier_semaphore()
    peers = [(sib, z)]
    peers += [(dev(y, x + d), z) for d in RING] + [(dev(y + d, x), z) for d in RING]
    for peer in peers:
        pl.semaphore_signal(barrier, inc=1, device_id=peer, device_id_type=MESH)
    for k in range(1, NZ):
        @pl.when(z + k < NZ)
        def _():
            pl.semaphore_signal(barrier, inc=1, device_id=(r, lax.rem(z + k, NZ)), device_id_type=MESH)

    for c in mine:
        c.wait()
    pl.semaphore_wait(barrier, len(peers) + z)
    for k in range(1, NZ):
        @pl.when(z + k >= NZ)
        def _():
            pl.semaphore_signal(ready, inc=1, device_id=(r, lax.rem(z + k, NZ)), device_id_type=MESH)

    started = []

    def copy(src, device, k):
        c = pltpu.make_async_remote_copy(
            src_ref=src, dst_ref=src, send_sem=send_sem.at[k], recv_sem=recv_sem.at[k],
            device_id=device, device_id_type=MESH,
        )
        started.append(c)
        return c

    def push(src, device, k):
        c = copy(src, device, k)
        c.start()
        return c

    counter = iter(range(1000))

    def key():
        return next(counter)

    def place(n, o, e):
        return dev(y + (o if n else e), x + (e if n else o))

    def slab(n, o, e):
        return col.at[n, pl.ds(place(n, o, e) * group_rows, group_rows)]

    ev = {}
    sib_copies = []

    def to_sib(n, o, e):
        sib_copies.append(push(slab(n, o, e), (sib, z), key()))

    def along_second(n, o):
        for e in RING:
            ev[n, o, e] = push(slab(n, o, 0), (place(n, 0, e), z), key())

    for d in RING:
        for n in range(2):
            ev[n, d] = push(slab(n, 0, 0), (place(n, d, 0), z), key())
    for n in range(2):
        along_second(n, 0)
    zev = [copy(row.at[z], (r, lax.rem(z + k, NZ)), key()) for k in range(1, NZ)]
    for k in range(1, NZ):
        @pl.when(z + k >= NZ)
        def _():
            zev[k - 1].start()

    for n in range(2):
        to_sib(n, 0, 0)

    i = lax.broadcasted_iota(jnp.int32, (BLK, BLK), 0)
    j = lax.broadcasted_iota(jnp.int32, (BLK, BLK), 1)
    base = jnp.exp(-jnp.abs(i - j).astype(F32) / TAPER_CELLS) * (1.0 / (members - 1))
    taper[0] = jnp.zeros((BLK, BLK), F32)
    for d in range(DISTS):
        taper[d + 1] = base * math.exp(-d / DIST_SCALE)
    col_blocks = col.shape[1]
    for c in listed:
        c.wait()
    lists[...] = slot_lists(pairs[0], pairs[1], pairs[2], count[0, 0], col_blocks)
    to_smem = pltpu.make_async_copy(lists, list_smem, local_sem.at[3 * group_rows + 4])
    to_smem.start()

    for d in RING:
        for n in range(2):
            ev[n, d].wait_recv()
            along_second(n, -d)
            to_sib(n, -d, 0)
    @pl.when(z < NZ - 1)
    def _():
        pl.semaphore_wait(ready, NZ - 1 - z)

    for k in range(1, NZ):
        @pl.when(z + k < NZ)
        def _():
            zev[k - 1].start()

    for o in (0,) + RING:
        for e in RING:
            for n in range(2):
                ev[n, -o, e].wait_recv()
                to_sib(n, -o, -e)
    for c in zev:
        c.wait_recv()
    to_smem.wait()
    for c in sib_copies:
        c.wait_recv()

    tn = (((0,), (0,)), ((), ()))

    def entry(a, s):
        e = list_smem[0, a * SLOTS + s]
        return e >> (col_blocks.bit_length() - 1), e & (col_blocks - 1)

    def target(t):
        half = NZ // 2
        low = z // half * half
        across = (half - low) + t + lax.rem(z, 2) * (1 - 2 * lax.rem(t, 2))
        near = low + lax.rem(z + t + 1, half)
        return jnp.where(t < half, across, near)

    @pl.loop(0, NZ)
    def _(t):
        g = target(t)
        turns = SLOTS // GROUP
        steps = turns * group_rows
        products, tapered, sums = {}, {}, {}
        for i in range(steps + 2):
            if i < steps:
                b = i // turns
                xa = row[g, b]
                entries = [entry(g * group_rows + b, i % turns * GROUP + n) for n in range(GROUP)]
                products[i] = entries, [
                    lax.dot_general(col[0, q], xa, tn, preferred_element_type=F32) for _, q in entries
                ]
            if 1 <= i <= steps:
                entries, prods = products.pop(i - 1)
                tapered[i - 1] = entries, jnp.concatenate(
                    [(p * taper[d]).astype(BF16) for p, (d, _) in zip(prods, entries)], axis=0
                )
            if i >= 2:
                b, turn = divmod(i - 2, turns)
                entries, weights = tapered.pop(i - 2)
                vb = jnp.concatenate([col[1, q] for _, q in entries], axis=1)
                term = jnp.dot(vb, weights, preferred_element_type=F32)
                sums[b] = term if turn == 0 else sums[b] + term
                if turn == turns - 1:
                    done = sums.pop(b)
                    own[b] = done
                    part[t, b] = done.astype(BF16)

        @pl.when(t < NZ - 1)
        def _():
            pltpu.make_async_remote_copy(
                src_ref=part.at[t], dst_ref=landed.at[z], send_sem=rs_send.at[t], recv_sem=rs_recv.at[z],
                device_id=(r, g), device_id_type=MESH,
            ).start()

    total = own[...]
    for k in range(1, NZ):
        source = lax.rem(z + k, NZ)
        done = pltpu.make_async_remote_copy(
            src_ref=part.at[k - 1], dst_ref=landed.at[source], send_sem=rs_send.at[k - 1],
            recv_sem=rs_recv.at[source], device_id=(r, source), device_id_type=MESH,
        )
        done.wait()
        total = total + landed[source].astype(F32)
    for b in range(group_rows):
        out_ref[:, b * BLK : (b + 1) * BLK] = total[b]
    for c in started:
        c.wait_send()


def local(anomalies, innovations, pair_rows, pair_cols, pair_dist, pair_counts):
    cells, members = anomalies.shape
    columns = innovations.shape[1]
    n_rows = lax.axis_size("rows")
    vm = pl.BlockSpec(memory_space=pltpu.VMEM)
    hbm = pl.BlockSpec(memory_space=pltpu.HBM)
    each = cells // BLK
    blocks = NZ * each
    operands = anomalies.T, innovations.T, pair_rows, pair_cols, pair_dist
    out = pl.pallas_call(
        kernel,
        out_shape=jax.ShapeDtypeStruct((columns, cells), F32),
        in_specs=[hbm] * 6,
        out_specs=vm,
        scratch_shapes=[
            pltpu.SMEM(pair_counts.shape, jnp.int32),
            pltpu.VMEM((3,) + pair_rows.shape, jnp.int32),
            pltpu.VMEM((2, n_rows * each, members, BLK), BF16),
            pltpu.VMEM((NZ, each, members, BLK), BF16),
            pltpu.VMEM((DISTS + 1, BLK, BLK), F32),
            pltpu.VMEM((1, blocks * SLOTS), jnp.int32),
            pltpu.SMEM((1, blocks * SLOTS), jnp.int32),
            pltpu.VMEM((NZ, each, columns, BLK), BF16),
            pltpu.VMEM((each, columns, BLK), F32),
            pltpu.VMEM((NZ, each, columns, BLK), BF16),
            pltpu.SemaphoreType.DMA((96,)),
            pltpu.SemaphoreType.DMA((96,)),
            pltpu.SemaphoreType.DMA((NZ - 1,)),
            pltpu.SemaphoreType.DMA((NZ,)),
            pltpu.SemaphoreType.DMA((3 * each + 5,)),
            pltpu.SemaphoreType.REGULAR,
        ],
        compiler_params=pltpu.CompilerParams(
            collective_id=0, has_side_effects=True, vmem_limit_bytes=40 << 20
        ),
        name="increment",
    )(pair_counts, *(pltpu.with_memory_space_constraint(o, pltpu.HBM) for o in operands))
    return out.T


def solution(mesh):
    split = P(("rows", "cols"), None)
    pairs = P("rows", "cols")
    return jax.shard_map(
        local, mesh=mesh, in_specs=(split, split, pairs, pairs, pairs, pairs), out_specs=split, check_vma=False
    )
```

```python
import functools
import math

import jax
import jax.numpy as jnp
from jax import lax
from jax.experimental import pallas as pl
from jax.experimental.pallas import tpu as pltpu
from jax.sharding import PartitionSpec as P

BLK = 128
SLOTS = 32
GROUP = 8
TAPER_CELLS = 8
DIST_SCALE = 4.0
DISTS = 8
NY, NX, NZ = 4, 4, 8
MESH = pl.DeviceIdType.MESH
RING = (1, -1, 2)
F32, BF16 = jnp.float32, jnp.bfloat16


def slot_lists(rows, cols, dist, count, col_blocks):
    slots = rows.shape[1]
    chunks = range(slots // BLK)
    live = lax.broadcasted_iota(jnp.int32, (1, slots), 1) < count
    held = jnp.where(live, rows, 2 * slots)
    entry = (dist + 1) * col_blocks + cols
    lane = lax.broadcasted_iota(jnp.int32, (BLK, BLK), 1)
    earlier = lax.broadcasted_iota(jnp.int32, (BLK, BLK), 0) < lane

    def part(v, c):
        return v[:, c * BLK : (c + 1) * BLK]

    def down(v, c):
        return jnp.broadcast_to(part(v, c), (BLK, BLK)).T

    held_down = [down(held, c) for c in chunks]
    places = []
    for c in chunks:
        same = jnp.where((held_down[c] == part(held, c)) & earlier, 1, 0)
        for e in range(c):
            same = same + jnp.where(held_down[e] == part(held, c), 1, 0)
        places.append(part(held, c) * SLOTS + jnp.sum(same, axis=0, keepdims=True))
    place = jnp.concatenate(places, axis=1)
    place_down = [down(place, c) for c in chunks]
    entry_down = [down(entry, c) for c in chunks]
    out = []
    for c in chunks:
        found = jnp.zeros((BLK, BLK), jnp.int32)
        for e in chunks:
            found = found + jnp.where(place_down[e] == lane + c * BLK, entry_down[e], 0)
        out.append(jnp.sum(found, axis=0, keepdims=True))
    return jnp.concatenate(out, axis=1)


def kernel(
    count_ref, x_ref, v_ref, rows_ref, cols_ref, dist_ref, out_ref,
    count, pairs, col, row, taper, lists, list_smem, part, own, landed,
    send_sem, recv_sem, rs_send, rs_recv, local_sem, ready,
):
    r, z = lax.axis_index("rows"), lax.axis_index("cols")
    core = lax.rem(r, 2)
    chip = r // 2
    x, y = lax.rem(chip, NX), chip // NX
    members, cells = x_ref.shape

    def dev(yy, xx):
        return (lax.rem(yy + NY, NY) * NX + lax.rem(xx + NX, NX)) * 2 + core

    sib = r + 1 - 2 * core

    barrier = pltpu.get_barrier_semaphore()
    peers = [(sib, z)]
    peers += [(dev(y, x + d), z) for d in RING] + [(dev(y + d, x), z) for d in RING]
    for peer in peers:
        pl.semaphore_signal(barrier, inc=1, device_id=peer, device_id_type=MESH)
    for k in range(1, NZ):
        @pl.when(z + k < NZ)
        def _():
            pl.semaphore_signal(barrier, inc=1, device_id=(r, lax.rem(z + k, NZ)), device_id_type=MESH)

    group_rows = cells // BLK
    mine = []
    own_blocks = pl.ds(r * group_rows, group_rows)
    copies_in = ((x_ref, col.at[0, own_blocks]), (v_ref, col.at[1, own_blocks]), (x_ref, row.at[z]))
    for n, (src, dst) in enumerate(copies_in):
        for b in range(group_rows):
            mine.append(
                pltpu.make_async_copy(
                    src.at[:, b * BLK : (b + 1) * BLK], dst.at[b], local_sem.at[n * group_rows + b]
                )
            )
    for c in mine:
        c.start()
    listed = [pltpu.make_async_copy(count_ref, count, local_sem.at[3 * group_rows])]
    for n, ref in enumerate((rows_ref, cols_ref, dist_ref)):
        listed.append(pltpu.make_async_copy(ref, pairs.at[n], local_sem.at[3 * group_rows + 1 + n]))
    for c in listed:
        c.start()

    for c in mine:
        c.wait()
    pl.semaphore_wait(barrier, len(peers) + z)
    for k in range(1, NZ):
        @pl.when(z + k >= NZ)
        def _():
            pl.semaphore_signal(ready, inc=1, device_id=(r, lax.rem(z + k, NZ)), device_id_type=MESH)

    started = []

    def copy(src, device, k):
        c = pltpu.make_async_remote_copy(
            src_ref=src, dst_ref=src, send_sem=send_sem.at[k], recv_sem=recv_sem.at[k],
            device_id=device, device_id_type=MESH,
        )
        started.append(c)
        return c

    def push(src, device, k):
        c = copy(src, device, k)
        c.start()
        return c

    counter = iter(range(1000))

    def key():
        return next(counter)

    def place(n, o, e):
        return dev(y + (o if n else e), x + (e if n else o))

    def slab(n, o, e):
        return col.at[n, pl.ds(place(n, o, e) * group_rows, group_rows)]

    ev = {}
    sib_copies = []

    def to_sib(n, o, e):
        sib_copies.append(push(slab(n, o, e), (sib, z), key()))

    def along_second(n, o):
        for e in RING:
            ev[n, o, e] = push(slab(n, o, 0), (place(n, 0, e), z), key())

    for d in RING:
        for n in range(2):
            ev[n, d] = push(slab(n, 0, 0), (place(n, d, 0), z), key())
    for n in range(2):
        along_second(n, 0)
    zev = [copy(row.at[z], (r, lax.rem(z + k, NZ)), key()) for k in range(1, NZ)]
    for k in range(1, NZ):
        @pl.when(z + k >= NZ)
        def _():
            zev[k - 1].start()

    for n in range(2):
        to_sib(n, 0, 0)

    i = lax.broadcasted_iota(jnp.int32, (BLK, BLK), 0)
    j = lax.broadcasted_iota(jnp.int32, (BLK, BLK), 1)
    base = jnp.exp(-jnp.abs(i - j).astype(F32) / TAPER_CELLS) * (1.0 / (members - 1))
    taper[0] = jnp.zeros((BLK, BLK), F32)
    for d in range(DISTS):
        taper[d + 1] = base * math.exp(-d / DIST_SCALE)
    col_blocks = col.shape[1]
    for c in listed:
        c.wait()
    lists[...] = slot_lists(pairs[0], pairs[1], pairs[2], count[0, 0], col_blocks)
    to_smem = pltpu.make_async_copy(lists, list_smem, local_sem.at[3 * group_rows + 4])
    to_smem.start()

    for d in RING:
        for n in range(2):
            ev[n, d].wait_recv()
            along_second(n, -d)
            to_sib(n, -d, 0)
    @pl.when(z < NZ - 1)
    def _():
        pl.semaphore_wait(ready, NZ - 1 - z)

    for k in range(1, NZ):
        @pl.when(z + k < NZ)
        def _():
            zev[k - 1].start()

    for o in (0,) + RING:
        for e in RING:
            for n in range(2):
                ev[n, -o, e].wait_recv()
                to_sib(n, -o, -e)
    for c in zev:
        c.wait_recv()
    to_smem.wait()
    for c in sib_copies:
        c.wait_recv()

    tn = (((0,), (0,)), ((), ()))

    def entry(a, s):
        e = list_smem[0, a * SLOTS + s]
        return e >> (col_blocks.bit_length() - 1), e & (col_blocks - 1)

    def target(t):
        half = NZ // 2
        low = z // half * half
        across = (half - low) + t + lax.rem(z, 2) * (1 - 2 * lax.rem(t, 2))
        near = low + lax.rem(z + t + 1, half)
        return jnp.where(t < half, across, near)

    @pl.loop(0, NZ)
    def _(t):
        g = target(t)
        turns = SLOTS // GROUP
        steps = turns * group_rows
        products, tapered, sums = {}, {}, {}
        for i in range(steps + 2):
            if i < steps:
                b = i // turns
                xa = row[g, b]
                entries = [entry(g * group_rows + b, i % turns * GROUP + n) for n in range(GROUP)]
                products[i] = entries, [
                    lax.dot_general(col[0, q], xa, tn, preferred_element_type=F32) for _, q in entries
                ]
            if 1 <= i <= steps:
                entries, prods = products.pop(i - 1)
                tapered[i - 1] = entries, jnp.concatenate(
                    [(p * taper[d]).astype(BF16) for p, (d, _) in zip(prods, entries)], axis=0
                )
            if i >= 2:
                b, turn = divmod(i - 2, turns)
                entries, weights = tapered.pop(i - 2)
                vb = jnp.concatenate([col[1, q] for _, q in entries], axis=1)
                term = jnp.dot(vb, weights, preferred_element_type=F32)
                sums[b] = term if turn == 0 else sums[b] + term
                if turn == turns - 1:
                    done = sums.pop(b)
                    own[b] = done
                    part[t, b] = done.astype(BF16)

        @pl.when(t < NZ - 1)
        def _():
            pltpu.make_async_remote_copy(
                src_ref=part.at[t], dst_ref=landed.at[z], send_sem=rs_send.at[t], recv_sem=rs_recv.at[z],
                device_id=(r, g), device_id_type=MESH,
            ).start()

    total = own[...]
    for k in range(1, NZ):
        source = lax.rem(z + k, NZ)
        done = pltpu.make_async_remote_copy(
            src_ref=part.at[k - 1], dst_ref=landed.at[source], send_sem=rs_send.at[k - 1],
            recv_sem=rs_recv.at[source], device_id=(r, source), device_id_type=MESH,
        )
        done.wait()
        total = total + landed[source].astype(F32)
    for b in range(group_rows):
        out_ref[:, b * BLK : (b + 1) * BLK] = total[b]
    for c in started:
        c.wait_send()


def local(anomalies, innovations, pair_rows, pair_cols, pair_dist, pair_counts):
    cells, members = anomalies.shape
    columns = innovations.shape[1]
    n_rows = lax.axis_size("rows")
    vm = pl.BlockSpec(memory_space=pltpu.VMEM)
    hbm = pl.BlockSpec(memory_space=pltpu.HBM)
    each = cells // BLK
    blocks = NZ * each
    operands = anomalies.T, innovations.T, pair_rows, pair_cols, pair_dist
    out = pl.pallas_call(
        kernel,
        out_shape=jax.ShapeDtypeStruct((columns, cells), F32),
        in_specs=[hbm] * 6,
        out_specs=vm,
        scratch_shapes=[
            pltpu.SMEM(pair_counts.shape, jnp.int32),
            pltpu.VMEM((3,) + pair_rows.shape, jnp.int32),
            pltpu.VMEM((2, n_rows * each, members, BLK), BF16),
            pltpu.VMEM((NZ, each, members, BLK), BF16),
            pltpu.VMEM((DISTS + 1, BLK, BLK), F32),
            pltpu.VMEM((1, blocks * SLOTS), jnp.int32),
            pltpu.SMEM((1, blocks * SLOTS), jnp.int32),
            pltpu.VMEM((NZ, each, columns, BLK), BF16),
            pltpu.VMEM((each, columns, BLK), F32),
            pltpu.VMEM((NZ, each, columns, BLK), BF16),
            pltpu.SemaphoreType.DMA((96,)),
            pltpu.SemaphoreType.DMA((96,)),
            pltpu.SemaphoreType.DMA((NZ - 1,)),
            pltpu.SemaphoreType.DMA((NZ,)),
            pltpu.SemaphoreType.DMA((3 * each + 5,)),
            pltpu.SemaphoreType.REGULAR,
        ],
        compiler_params=pltpu.CompilerParams(
            collective_id=0, has_side_effects=True, vmem_limit_bytes=40 << 20
        ),
        name="increment",
    )(pair_counts, *(pltpu.with_memory_space_constraint(o, pltpu.HBM) for o in operands))
    return out.T


def solution(mesh):
    split = P(("rows", "cols"), None)
    pairs = P("rows", "cols")
    return jax.shard_map(
        local, mesh=mesh, in_specs=(split, split, pairs, pairs, pairs, pairs), out_specs=split, check_vma=False
    )
```
